256 devices in a mesh: dp: 4 (over z_hi, core), expert: 64 (over x, y, z_lo).
Axes of the slice: x: 4, y: 4, z: 8 (z_hi: 2, z_lo: 4; z = z_hi * 4 + z_lo), core: 2. Of those that a mesh axis runs over, the one named last changes fastest.
Arguments:
- frames: bfloat16 [32768, 1024], P(('dp', 'expert')), may hold values from -6 to 6
- lengths: int32 [4], P('dp'), may hold values from 4096 to 8192
- expert_ids: int32 [32768, 2], P(('dp', 'expert')), may hold values from 0 to 63, all different within a row; in each aligned block of 128 rows (0 to 127, 128 to 255, ...) at most 8 rows name the same one
- capacity: int32 [64], replicated, may hold values from 4 to 8
- resident: int32 [64], replicated, may hold values from 0 to 63, each once
- partner: int32 [64], replicated, may hold values from 0 to 63, as said below
- conv_gain: float32 [1024], replicated, may hold values from 0.5 to 1.5
- conv_kernel: float32 [31, 1024], replicated, may hold values from -1 to 1
- conv_bias: float32 [1024], replicated, may hold values from -3 to 3
- ffn_gain: float32 [1024], replicated, may hold values from 0.5 to 1.5
- router: bfloat16 [1024, 64], replicated, may hold values from -0.1875 to 0.1875
- gate_weight: bfloat16 [64, 1024, 2048], P('expert', None, 'dp'), may hold values from -4 to 4
- up_weight: bfloat16 [64, 1024, 2048], P('expert', None, 'dp'), may hold values from -4 to 4
- down_weight: bfloat16 [64, 1024, 2048], P('expert', None, 'dp'), may hold values from -4 to 4
- gate_mean_grad: bfloat16 [64, 1024, 2048], P('expert', None, 'dp'), may hold values from -4 to 4
- gate_mean_square: bfloat16 [64, 1024, 2048], P('expert', None, 'dp'), may hold values from 0.25 to 4
- up_mean_grad: bfloat16 [64, 1024, 2048], P('expert', None, 'dp'), may hold values from -4 to 4
- up_mean_square: bfloat16 [64, 1024, 2048], P('expert', None, 'dp'), may hold values from 0.25 to 4
- down_mean_grad: bfloat16 [64, 1024, 2048], P('expert', None, 'dp'), may hold values from -4 to 4
- down_mean_square: bfloat16 [64, 1024, 2048], P('expert', None, 'dp'), may hold values from 0.25 to 4
Outputs:
- block_out: bfloat16 [32768, 1024], P(('dp', 'expert'))
- fresh_gate: bfloat16 [64, 1024, 2048], P('expert', None, 'dp')
- fresh_up: bfloat16 [64, 1024, 2048], P('expert', None, 'dp')
- fresh_down: bfloat16 [64, 1024, 2048], P('expert', None, 'dp')
The draws below stay inside these ranges and needn't reach their ends.
Inputs may be any that keep to these rules, and one draw needn't show every extreme that they name: `expert_ids`: in each aligned block of 128 frames (the frames of one device) no expert is named by more than 8 choices, a bound that some block reaches. A pairing of the slots: partner[partner[d]] = d and partner[d] != d. `resident`: A permutation of the experts.
All inputs are finite; a program needn't handle non-finite values.
Results may differ from the reference program's by a relative error of at most 0.007.
Values may be sent and summed in bfloat16 or wider, within the bound.
A program may use at most 128 MiB of HBM per device.

```python
import math
import jax
import jax.numpy as jnp
import numpy as np
from jax import lax

D = 1024
FF = 2048
K = 31
TOP = 2
TOK_DEV = 128
LENGTH = 8192
EXPERTS = 64
CAP = 8
TOKENS = 32768
SEQS = 4


def draw_lengths(key, part):
    values = jax.random.randint(key, (SEQS,), LENGTH // 2, LENGTH + 1)
    chosen_index = jax.random.randint(jax.random.fold_in(key, 7), (), 0, SEQS)
    return jnp.where(jnp.arange(SEQS) == chosen_index, LENGTH, values).astype(jnp.int32)


def draw_capacity(key, part):
    values = jax.random.randint(key, (EXPERTS,), (CAP + 1) // 2, CAP + 1)
    chosen_index = jax.random.randint(jax.random.fold_in(key, 11), (), 0, EXPERTS)
    return jnp.where(jnp.arange(EXPERTS) == chosen_index, CAP, values).astype(jnp.int32)


def draw_partner(key, part):
    shuffled = jax.random.permutation(key, EXPERTS)
    leaders = shuffled[0::2]
    members = shuffled[1::2]
    result = jnp.zeros((EXPERTS,), jnp.int32).at[leaders].set(members.astype(jnp.int32))
    result = result.at[members].set(leaders.astype(jnp.int32))
    return result


def block_levels(own_key, extent, shards, least, largest):
    level = 1.0
    for dim, blocks in shards:
        steps = jax.random.uniform(jax.random.fold_in(jax.random.fold_in(own_key, 6), dim), (blocks,), jnp.float32, least / len(shards), largest / len(shards))
        level = level * jnp.repeat(jnp.exp(steps), extent[dim] // blocks).reshape((-1,) + (1,) * (len(extent) - 1 - dim))
    return level


def routed_block(stream_key, own, number, rows, count, top, reach, lean):
    sequence = jax.random.permutation(stream_key, count)
    crowded, common = load_shares(count, rows * top, reach, lean, True), load_shares(count, rows * top, reach, lean, False)
    places = jnp.arange(count)

    def named(sizes, rotation):
        used = int((sizes > 0).sum())
        fixed = max(1, used // 4)
        shifted = fixed + (places - fixed + rotation * (used - fixed)) % max(1, count - fixed)
        return jnp.zeros((count,), jnp.int32).at[sequence[jnp.where(places < fixed, places, shifted)]].set(jnp.asarray(sizes, jnp.int32))

    sizes = jnp.where(number % 4 == 0, named(crowded, number // 4), named(common, number - number // 4 - 1))
    mixed = jax.random.permutation(jax.random.fold_in(own, 3), count)
    donor, taker = mixed[0:count // 2 * 2:2], mixed[1:count // 2 * 2:2]
    slack = jnp.minimum(sizes[donor] - 1, reach - sizes[taker]) // 2
    slack = jnp.where((donor == sequence[0]) | (taker == sequence[0]) | (sizes[taker] == 0), 0, jnp.maximum(slack, 0))
    shifted = jax.random.randint(jax.random.fold_in(own, 4), (count // 2,), 0, 1 << 20) % (slack + 1)
    sizes = sizes.at[donor].add(-shifted).at[taker].add(shifted)
    items = jnp.searchsorted(jnp.cumsum(sizes), jnp.arange(rows * top), side="right").astype(jnp.int32)
    grid = items.reshape(top, rows).T
    grid = grid[jax.random.permutation(jax.random.fold_in(own, 1), rows)]
    rotation = jax.random.randint(jax.random.fold_in(own, 2), (rows, 1), 0, top)
    return jnp.take_along_axis(grid, (jnp.arange(top)[None, :] + rotation) % top, axis=1)


def load_shares(number_of, total, bound, skew, full):
    loads = [(1 << 20) // math.isqrt(standing ** skew) + 1 for standing in range(1, number_of + 1)]
    largest = bound if full else min(bound, max(-(-total // number_of), total * loads[0] // sum(loads)))
    least = 1 if total - largest >= number_of - 1 else 0
    counts, rest = [largest] + [least] * (number_of - 1), total - largest - least * (number_of - 1)
    while rest > 0:
        free = [i for i in range(1, number_of) if counts[i] < largest] or [i for i in range(1, number_of) if counts[i] < bound]
        mass, remaining = sum([loads[i] for i in free]), rest
        for i in free:
            more = min(bound - counts[i], max(1, remaining * loads[i] // mass), rest)
            counts[i] = counts[i] + more
            rest = rest - more
    return np.array(counts)


def noise(rng, extent, deviation, reach, pieces=(), kind=jnp.bfloat16):
    level = block_levels(rng, extent, pieces, -0.22, 0.18) if pieces else 1.0
    values = jax.random.normal(rng, extent, jnp.float32) * deviation * level
    return jnp.minimum(jnp.maximum(values, -reach), reach).astype(kind)


def setup_inputs(seed: int = 0) -> dict:
    key_list = jax.random.split(jax.random.key(seed), 21)
    frames = noise(key_list[0], (TOKENS, D), 1.0, 6.0, ((0, 256),))
    lengths = draw_lengths(jax.random.fold_in(key_list[20], 71), 0)
    expert_ids_keys = jax.random.split(jax.random.fold_in(key_list[2], 1), TOKENS // TOK_DEV)
    expert_ids_turns = jax.random.permutation(jax.random.fold_in(key_list[2], 3), TOKENS // TOK_DEV)
    expert_ids = jax.vmap(lambda own, number: routed_block(jax.random.fold_in(key_list[2], 2), own, number, TOK_DEV, EXPERTS, TOP, CAP, 2))(expert_ids_keys, expert_ids_turns).reshape((TOKENS, TOP))
    capacity = draw_capacity(jax.random.fold_in(key_list[20], 71), 0)
    resident = jax.random.permutation(key_list[4], EXPERTS).astype(jnp.int32)
    partner = draw_partner(jax.random.fold_in(key_list[20], 71), 0)
    conv_gain = jnp.clip(1.0 + 0.1 * jax.random.normal(key_list[6], (D,), jnp.float32), 0.5, 1.5)
    conv_kernel = noise(key_list[7], (K, D), K ** -0.5, 1.0, (), jnp.float32)
    conv_bias = noise(key_list[8], (D,), 0.5, 3.0, (), jnp.float32)
    ffn_gain = jnp.clip(1.0 + 0.1 * jax.random.normal(key_list[9], (D,), jnp.float32), 0.5, 1.5)
    router = noise(key_list[10], (D, EXPERTS), D ** -0.5, 0.1875)
    gate_weight = noise(key_list[11], (EXPERTS, D, FF), 1.0, 4.0, ((0, 64), (2, 4)))
    up_weight = noise(key_list[12], (EXPERTS, D, FF), 1.0, 4.0, ((0, 64), (2, 4)))
    down_weight = noise(key_list[13], (EXPERTS, D, FF), 1.0, 4.0, ((0, 64), (2, 4)))
    gate_mean_grad = noise(key_list[14], (EXPERTS, D, FF), 1.0, 4.0, ((0, 64), (2, 4)))
    gate_mean_square = jnp.clip(jnp.exp(math.log(4.0) - 2.7725887 * jax.random.uniform(key_list[15], (EXPERTS, D, FF), jnp.float32) ** block_levels(key_list[15], (EXPERTS, D, FF), ((0, 64), (2, 4)), -0.2, 0.2)), 0.25, 4.0).astype(jnp.bfloat16)
    up_mean_grad = noise(key_list[16], (EXPERTS, D, FF), 1.0, 4.0, ((0, 64), (2, 4)))
    up_mean_square = jnp.clip(jnp.exp(math.log(4.0) - 2.7725887 * jax.random.uniform(key_list[17], (EXPERTS, D, FF), jnp.float32) ** block_levels(key_list[17], (EXPERTS, D, FF), ((0, 64), (2, 4)), -0.2, 0.2)), 0.25, 4.0).astype(jnp.bfloat16)
    down_mean_grad = noise(key_list[18], (EXPERTS, D, FF), 1.0, 4.0, ((0, 64), (2, 4)))
    down_mean_square = jnp.clip(jnp.exp(math.log(4.0) - 2.7725887 * jax.random.uniform(key_list[19], (EXPERTS, D, FF), jnp.float32) ** block_levels(key_list[19], (EXPERTS, D, FF), ((0, 64), (2, 4)), -0.2, 0.2)), 0.25, 4.0).astype(jnp.bfloat16)
    return dict(frames=frames, lengths=lengths, expert_ids=expert_ids, capacity=capacity, resident=resident, partner=partner, conv_gain=conv_gain, conv_kernel=conv_kernel, conv_bias=conv_bias, ffn_gain=ffn_gain, router=router, gate_weight=gate_weight, up_weight=up_weight, down_weight=down_weight, gate_mean_grad=gate_mean_grad, gate_mean_square=gate_mean_square, up_mean_grad=up_mean_grad, up_mean_square=up_mean_square, down_mean_grad=down_mean_grad, down_mean_square=down_mean_square)


LEARNING_RATE = 0.1
ADAM_EPSILON = 1e-08
NORM_EPSILON = 1e-05

def layer_norm(values, gain_row):
    centred = values - lax.optimization_barrier(jnp.mean(values, axis=-1, keepdims=True))
    variance = lax.optimization_barrier(jnp.mean(centred * centred, axis=-1, keepdims=True))
    return centred * lax.rsqrt(variance + NORM_EPSILON) * gain_row

def refresh(weight, first_moment, second_moment):
    step_size = LEARNING_RATE * first_moment.astype(jnp.float32) / (jnp.sqrt(second_moment.astype(jnp.float32)) + ADAM_EPSILON)
    return (weight.astype(jnp.float32) - step_size).astype(jnp.bfloat16)

def expert_part(inputs, gate_block, up_block, down_block):
    gate_pre = jnp.dot(inputs, gate_block, preferred_element_type=jnp.float32) * D ** (-0.5)
    up_pre = jnp.dot(inputs, up_block, preferred_element_type=jnp.float32) * D ** (-0.5)
    hidden = (jax.nn.silu(gate_pre) * up_pre).astype(jnp.bfloat16)
    return lax.dot_general(hidden, down_block, (((1,), (1,)), ((), ())), preferred_element_type=jnp.float32) * FF ** (-0.5)

def reference(frames, lengths, expert_ids, capacity, resident, partner, conv_gain, conv_kernel, conv_bias, ffn_gain, router, gate_weight, up_weight, down_weight, gate_mean_grad, gate_mean_square, up_mean_grad, up_mean_square, down_mean_grad, down_mean_square):
    inputs_f = frames.astype(jnp.float32)
    frame_iota = jnp.arange(TOKENS, dtype=jnp.int32)
    utterance = frame_iota // LENGTH
    offsets = frame_iota % LENGTH
    live_rows = (offsets < lengths[utterance]).astype(jnp.float32)[:, None]
    normed = (layer_norm(inputs_f, conv_gain) * live_rows).astype(jnp.bfloat16)
    margin = (K - 1) // 2
    grouped = normed.astype(jnp.float32).reshape(SEQS, LENGTH, D)
    widened = jnp.pad(grouped, ((0, 0), (margin, margin), (0, 0)))
    conv_sum = jnp.zeros((SEQS, LENGTH, D), jnp.float32)
    for tap_index in range(K):
        conv_sum = conv_sum + conv_kernel[tap_index] * widened[:, tap_index:tap_index + LENGTH]
    conv_sum = conv_sum.reshape(TOKENS, D)
    mixed_rows = (inputs_f + live_rows * jax.nn.silu(conv_sum + conv_bias)).astype(jnp.bfloat16)
    ffn_in = layer_norm(mixed_rows.astype(jnp.float32), ffn_gain).astype(jnp.bfloat16)
    logits = jnp.dot(ffn_in, router, preferred_element_type=jnp.float32)
    chosen = jnp.take_along_axis(logits, expert_ids, axis=1)
    scores = jax.nn.sigmoid(chosen)
    gate_values = (scores / lax.optimization_barrier(jnp.sum(scores, axis=-1, keepdims=True))).astype(jnp.bfloat16)
    fresh_gate = refresh(gate_weight[partner], gate_mean_grad[partner], gate_mean_square[partner])
    fresh_up = refresh(up_weight[partner], up_mean_grad[partner], up_mean_square[partner])
    fresh_down = refresh(down_weight[partner], down_mean_grad[partner], down_mean_square[partner])
    slot_iota = jnp.arange(EXPERTS, dtype=jnp.int32)
    holder = resident[partner]
    new_slot = jnp.zeros((EXPERTS,), jnp.int32).at[holder].set(slot_iota)
    block_count = TOKENS // TOK_DEV
    block_ids = expert_ids.reshape(block_count, TOP * TOK_DEV)
    onehot = (block_ids[:, :, None] == slot_iota[None, None, :]).astype(jnp.int32)
    earlier = jnp.cumsum(onehot, axis=1) - onehot
    rank_in_block = lax.optimization_barrier(jnp.sum(earlier * onehot, axis=-1))
    kept_pairs = rank_in_block < capacity[block_ids]
    per_expert = block_count * CAP
    slot_index = block_ids * per_expert + jnp.arange(block_count, dtype=jnp.int32)[:, None] * CAP + rank_in_block
    slot_index = jnp.where(kept_pairs, slot_index, EXPERTS * per_expert).reshape(-1)
    kept_flat = kept_pairs.reshape(-1)
    pair_rows = jnp.repeat(ffn_in, TOP, axis=0)
    buffer = jnp.zeros((EXPERTS * per_expert, D), jnp.bfloat16).at[slot_index].set(pair_rows, mode='drop')

    def run_expert(packed):
        rows_in, slot_of = packed
        return expert_part(rows_in, fresh_gate[slot_of], fresh_up[slot_of], fresh_down[slot_of]).astype(jnp.bfloat16)
    expert_out = lax.map(run_expert, (buffer.reshape(EXPERTS, per_expert, D), new_slot))
    expert_flat = expert_out.reshape(EXPERTS * per_expert, D)
    fetched = expert_flat[jnp.minimum(slot_index, EXPERTS * per_expert - 1)]
    fetched = jnp.where(kept_flat[:, None], fetched.astype(jnp.float32), 0.0)
    weighted = gate_values.astype(jnp.float32).reshape(-1)[:, None] * fetched
    moe_sum = lax.optimization_barrier(jnp.sum(weighted.reshape(TOKENS, TOP, D), axis=1))
    block_out = (mixed_rows.astype(jnp.float32) + 0.5 * moe_sum).astype(jnp.bfloat16)
    return (block_out, fresh_gate, fresh_up, fresh_down)
```

```python
import functools

import jax
import jax.numpy as jnp
from jax import lax
from jax.experimental import pallas as pl
from jax.experimental.pallas import tpu as pltpu
from jax.sharding import PartitionSpec as P

D = 1024
FF = 2048
K = 31


LEARNING_RATE = 0.1
ADAM_EPSILON = 1e-08
NORM_EPSILON = 1e-05

MESH = pl.DeviceIdType.MESH
XY = 16
ZL = 4
ZN = 8
HALF = ZN // 2
GROUP = XY * ZL
SLOTS = 8
TOK = 128
FLOC = 512
ROWS = XY * 2 * SLOTS
PIECE = D // GROUP


def extended(cells, sides, width):
    for axis, dim in sides:
        count = lax.axis_size(axis)
        ends = count - 1
        head = lax.slice_in_dim(cells, 0, width, axis=dim)
        tail = lax.slice_in_dim(cells, cells.shape[dim] - width, cells.shape[dim], axis=dim)
        cells = jnp.concatenate(
            [
                lax.ppermute(tail, axis, [(i, (i + 1) % count) for i in range(ends)]),
                cells,
                lax.ppermute(head, axis, [((i + 1) % count, i) for i in range(ends)]),
            ],
            axis=dim,
        )
    return cells


def layer_norm(values, gain_row):
    centred = values - jnp.mean(values, axis=-1, keepdims=True)
    variance = jnp.mean(centred * centred, axis=-1, keepdims=True)
    return centred * lax.rsqrt(variance + NORM_EPSILON) * gain_row


def refresh(weight, first_moment, second_moment):
    step_size = (
        LEARNING_RATE
        * first_moment.astype(jnp.float32)
        / (jnp.sqrt(second_moment.astype(jnp.float32)) + ADAM_EPSILON)
    )
    return (weight.astype(jnp.float32) - step_size).astype(jnp.bfloat16)


def silu(value):
    return value / (1.0 + jnp.exp(-value))


def kernel(
    partner_ref,
    ffn_ref,
    mixed_ref,
    meta_ref,
    gw, gm, gs, uw, um, us, dw, dm, ds,
    out_ref,
    fg_ref,
    fu_ref,
    fd_ref,
    win,
    fresh,
    got0,
    got1,
    got2,
    arr,
    agx,
    agm,
    pbuf,
    prow,
    orow,
    yown,
    yoth,
    yin,
    yret,
    rret,
    part,
    rs_out,
    rs_in,
    load_sem,
    self_sem,
    self2_sem,
    send1,
    recv1,
    send2,
    recv2,
    ring_send,
    ring_recv,
    meta_send,
    meta_recv,
    plane_send,
    plane_recv,
    plane_self,
    x_send,
    x_recv,
    y_send,
    y_recv,
    ret_send,
    ret_recv,
    ret_self,
    rs_send,
    rs_recv,
):
    a = lax.axis_index("dp")
    e = lax.axis_index("expert")
    core = a % 2
    zlo = e % ZL
    xy = e // ZL
    z = (a // 2) * ZL + zlo

    def line(position):
        return ((position // ZL) * 2 + core, xy * ZL + position % ZL)

    def plane(spot):
        return (a, spot * ZL + zlo)

    partner_core = ((a // 2) * 2 + 1 - core, e)

    barrier = pltpu.get_barrier_semaphore()

    def greet_group(i, _):
        pl.semaphore_signal(barrier, inc=1, device_id=(a, (e + i) % GROUP), device_id_type=MESH)
        return _

    lax.fori_loop(1, GROUP, greet_group, 0)

    def greet_line(i, _):
        far = (1 - a // 2) * ZL + i
        pl.semaphore_signal(barrier, inc=1, device_id=line(far), device_id_type=MESH)
        return _

    lax.fori_loop(0, ZL, greet_line, 0)
    pl.semaphore_signal(barrier, inc=1, device_id=partner_core, device_id_type=MESH)

    sources = (gw, gm, gs, uw, um, us, dw, dm, ds)
    loads = [
        pltpu.make_async_copy(sources[i], win.at[i], load_sem.at[i]) for i in range(9)
    ]
    for copy in loads:
        copy.start()
    agx[z] = ffn_ref[...]
    agm[z] = meta_ref[...]
    pl.semaphore_wait(barrier, GROUP + ZL)

    def ring(step, way):
        if way == 0:
            block = (z - step + 1 + ZN) % ZN
            target = line((z + 1) % ZN)
        else:
            block = (z + step - 1) % ZN
            target = line((z - 1 + ZN) % ZN)
        if step == HALF:
            view = agx.at[block, pl.ds(way * (TOK // 2), TOK // 2)]
        else:
            view = agx.at[block]
        return pltpu.make_async_remote_copy(
            src_ref=view,
            dst_ref=view,
            send_sem=ring_send.at[way, step - 1],
            recv_sem=ring_recv.at[way, step - 1],
            device_id=target,
            device_id_type=MESH,
        )

    def ring_arrival(step, way):
        if way == 0:
            block = (z - step + ZN) % ZN
        else:
            block = (z + step) % ZN
        if step == HALF:
            view = agx.at[block, pl.ds(way * (TOK // 2), TOK // 2)]
        else:
            view = agx.at[block]
        pltpu.make_async_copy(view, view, ring_recv.at[way, step - 1]).wait()

    for way in range(2):
        ring(1, way).start()

    def meta_copy(i):
        return pltpu.make_async_remote_copy(
            src_ref=meta_ref,
            dst_ref=agm.at[z],
            send_sem=meta_send,
            recv_sem=meta_recv,
            device_id=line((z + i) % ZN),
            device_id_type=MESH,
        )

    def send_meta(i, _):
        meta_copy(i).start()
        return _

    lax.fori_loop(1, ZN, send_meta, 0)

    gots = (got0, got1, got2)
    outs = (fg_ref, fu_ref, fd_ref)

    def refresh_chunk(k):
        for i in range(3):
            loads[3 * k + i].wait()

        def tile(i, _):
            rows = pl.ds(pl.multiple_of(i * 32, 32), 32)
            fresh[k, rows, :] = refresh(
                win[3 * k, rows, :], win[3 * k + 1, rows, :], win[3 * k + 2, rows, :]
            )
            return _

        lax.fori_loop(0, D // 32, tile, 0)

    def piece_target(i):
        other = ((xy // 4 + i // 16) % 4) * 16 + ((xy % 4 + (i // 4) % 4) % 4) * 4 + (zlo + i % 4) % 4
        return other

    def scatter_chunk(k):
        def send(i, _):
            other = piece_target(i)
            pltpu.make_async_remote_copy(
                src_ref=fresh.at[k, pl.ds(pl.multiple_of(other * PIECE, PIECE), PIECE)],
                dst_ref=gots[k].at[e],
                send_sem=send1.at[k],
                recv_sem=recv1.at[k],
                device_id=(a, other),
                device_id_type=MESH,
            ).start()
            return _

        pltpu.make_async_copy(
            fresh.at[k, pl.ds(pl.multiple_of(e * PIECE, PIECE), PIECE)], gots[k].at[e], self_sem.at[k]
        ).start()
        lax.fori_loop(1, GROUP, send, 0)

    def regroup_chunk(k):
        got = gots[k]
        bulk = got.at[pl.ds(0, GROUP - 1)]
        pltpu.make_async_copy(bulk, bulk, recv1.at[k]).wait()
        pltpu.make_async_copy(
            fresh.at[k, pl.ds(pl.multiple_of(e * PIECE, PIECE), PIECE)], got.at[e], self_sem.at[k]
        ).wait()

        def pick(i, _):
            arr[k, i] = got[partner_ref[i]]
            return _

        lax.fori_loop(0, GROUP, pick, 0)

        mine = outs[k].at[pl.ds(pl.multiple_of(e * PIECE, PIECE), PIECE)]
        pltpu.make_async_copy(arr.at[k, e], mine, self2_sem.at[k]).start()

        def send(i, _):
            other = piece_target(i)
            pltpu.make_async_remote_copy(
                src_ref=arr.at[k, other],
                dst_ref=mine,
                send_sem=send2.at[k],
                recv_sem=recv2.at[k],
                device_id=(a, other),
                device_id_type=MESH,
            ).start()
            return _

        lax.fori_loop(1, GROUP, send, 0)

    def pair_blocks(p):
        first = (z - (p + 1) % HALF + ZN) % ZN
        second = (z + 1 + p) % ZN
        return first, second

    def choices(p):
        first, second = pair_blocks(p)
        ma, mb = agm[first], agm[second]
        row = lax.broadcasted_iota(jnp.int32, (ROWS, 1), 0)
        column = lax.broadcasted_iota(jnp.int32, (1, 2 * TOK), 1)
        code = (zlo * (XY * SLOTS) + (row // (2 * SLOTS)) * SLOTS + row % SLOTS).astype(jnp.float32)
        same = (row // SLOTS) % 2 == column // TOK
        both = jnp.concatenate([ma, mb], axis=1)
        hit0 = (both[0:1] == code) & same
        hit1 = (both[1:2] == code) & same
        return hit0, hit1, both

    def dispatch(p):
        first, second = pair_blocks(p)
        hit0, hit1, _ = choices(p)
        select = jnp.where(hit0 | hit1, 1.0, 0.0).astype(jnp.bfloat16)
        rows = jnp.dot(select[:, :TOK], agx[first], preferred_element_type=jnp.float32)
        rows = rows + jnp.dot(select[:, TOK:], agx[second], preferred_element_type=jnp.float32)
        pbuf[p] = rows.astype(jnp.bfloat16)
        mine = prow.at[p, pl.ds(pl.multiple_of(xy * 2 * SLOTS, 2 * SLOTS), 2 * SLOTS)]
        pltpu.make_async_copy(
            pbuf.at[p, pl.ds(pl.multiple_of(xy * 2 * SLOTS, 2 * SLOTS), 2 * SLOTS)], mine, plane_self.at[p]
        ).start()

        def send(i, _):
            spot = (xy + i) % XY
            pltpu.make_async_remote_copy(
                src_ref=pbuf.at[p, pl.ds(pl.multiple_of(spot * 2 * SLOTS, 2 * SLOTS), 2 * SLOTS)],
                dst_ref=mine,
                send_sem=plane_send.at[p],
                recv_sem=plane_recv.at[p],
                device_id=plane(spot),
                device_id_type=MESH,
            ).start()
            return _

        lax.fori_loop(1, XY, send, 0)

    BULK = pl.ds(0, ROWS - 2 * SLOTS)
    OWN = pl.ds(pl.multiple_of(xy * 2 * SLOTS, 2 * SLOTS), 2 * SLOTS)

    refresh_chunk(0)
    scatter_chunk(0)
    for p in range(HALF):
        for way in range(2):
            ring_arrival(p + 1, way)
        if p + 2 <= HALF:
            for way in range(2):
                ring(p + 2, way).start()
        if p == 0:
            line_meta = agm.at[pl.ds(0, ZN - 1)]
            pltpu.make_async_copy(line_meta, line_meta, meta_recv).wait()
        dispatch(p)
        if p + 1 < 3:
            refresh_chunk(p + 1)
            scatter_chunk(p + 1)

    regroup_chunk(0)

    def expert_part(rows):
        gate_pre = jnp.dot(rows, fresh[0], preferred_element_type=jnp.float32) * D ** (-0.5)
        up_pre = jnp.dot(rows, fresh[1], preferred_element_type=jnp.float32) * D ** (-0.5)
        hidden = (silu(gate_pre) * up_pre).astype(jnp.bfloat16)
        return lax.dot_general(
            hidden, fresh[2], (((1,), (1,)), ((), ())), preferred_element_type=jnp.float32
        ) * FF ** (-0.5)

    def exchange(src, dst, p, send, recv):
        return pltpu.make_async_remote_copy(
            src_ref=src.at[p],
            dst_ref=dst.at[p],
            send_sem=send.at[p],
            recv_sem=recv.at[p],
            device_id=partner_core,
            device_id_type=MESH,
        )

    def settle(p):
        exchange(yoth, yin, p, y_send, y_recv).wait_recv()
        yret[p] = (yown[p] + yin[p].astype(jnp.float32)).astype(jnp.bfloat16)
        pltpu.make_async_copy(yret.at[p, OWN], rret.at[p, OWN], ret_self.at[p]).start()

        def send(i, _):
            spot = (xy + i) % XY
            pltpu.make_async_remote_copy(
                src_ref=yret.at[p, pl.ds(pl.multiple_of(spot * 2 * SLOTS, 2 * SLOTS), 2 * SLOTS)],
                dst_ref=rret.at[p, OWN],
                send_sem=ret_send.at[p],
                recv_sem=ret_recv.at[p],
                device_id=plane(spot),
                device_id_type=MESH,
            ).start()
            return _

        lax.fori_loop(1, XY, send, 0)

    def experts(p, _):
        bulk = prow.at[p, BULK]
        pltpu.make_async_copy(bulk, bulk, plane_recv.at[p]).wait()
        pltpu.make_async_copy(pbuf.at[p, OWN], prow.at[p, OWN], plane_self.at[p]).wait()
        exchange(prow, orow, p, x_send, x_recv).start()
        yown[p] = expert_part(prow[p])
        exchange(prow, orow, p, x_send, x_recv).wait_recv()
        yoth[p] = expert_part(orow[p]).astype(jnp.bfloat16)
        exchange(yoth, yin, p, y_send, y_recv).start()

        @pl.when(p > 0)
        def _settle():
            settle(p - 1)

        return _

    lax.fori_loop(0, HALF, experts, 0)
    settle(HALF - 1)
    regroup_chunk(1)

    def combine(p, _):
        bulk = rret.at[p, BULK]
        pltpu.make_async_copy(bulk, bulk, ret_recv.at[p]).wait()
        pltpu.make_async_copy(yret.at[p, OWN], rret.at[p, OWN], ret_self.at[p]).wait()
        first, second = pair_blocks(p)
        hit0, hit1, both = choices(p)
        weights = jnp.where(hit0, both[2:3], 0.0) + jnp.where(hit1, both[3:4], 0.0)
        weights = weights.T.astype(jnp.bfloat16)
        total = jnp.dot(weights, rret[p], preferred_element_type=jnp.float32)
        part[first] = total[:TOK]
        part[second] = total[TOK:]
        return _

    lax.fori_loop(0, HALF, combine, 0)

    def rs_view(ref, step, way):
        if step == 1:
            return ref.at[way, step - 1, pl.ds(way * (TOK // 2), TOK // 2)]
        return ref.at[way, step - 1]

    def rs(step, way):
        target = line((z + 1) % ZN) if way == 0 else line((z - 1 + ZN) % ZN)
        return pltpu.make_async_remote_copy(
            src_ref=rs_view(rs_out, step, way),
            dst_ref=rs_view(rs_in, step, way),
            send_sem=rs_send.at[way, step - 1],
            recv_sem=rs_recv.at[way, step - 1],
            device_id=target,
            device_id_type=MESH,
        )

    for step in range(1, HALF + 1):
        for way in range(2):
            distance = HALF + 1 - step
            owner = (z + distance) % ZN if way == 0 else (z - distance + ZN) % ZN
            half = pl.ds(way * (TOK // 2), TOK // 2)
            other_half = pl.ds((1 - way) * (TOK // 2), TOK // 2)
            if step > 1:
                rs(step - 1, way).wait_recv()
            if step == 1:
                rs_out[way, 0, half, :] = part[owner, half, :].astype(jnp.bfloat16)
            elif step == 2:
                rs_out[way, 1, half, :] = (
                    part[owner, half, :] + rs_in[way, 0, half, :].astype(jnp.float32)
                ).astype(jnp.bfloat16)
                rs_out[way, 1, other_half, :] = part[owner, other_half, :].astype(jnp.bfloat16)
            else:
                rs_out[way, step - 1] = (
                    part[owner] + rs_in[way, step - 2].astype(jnp.float32)
                ).astype(jnp.bfloat16)
            rs(step, way).start()
        if step == 1:
            regroup_chunk(2)
    for way in range(2):
        rs(HALF, way).wait_recv()
    moe = (
        part[z]
        + rs_in[0, HALF - 1].astype(jnp.float32)
        + rs_in[1, HALF - 1].astype(jnp.float32)
    )
    out_ref[...] = (mixed_ref[...].astype(jnp.float32) + 0.5 * moe).astype(jnp.bfloat16)

    for way in range(2):
        for step in range(1, HALF + 1):
            ring(step, way).wait_send()
            rs(step, way).wait_send()
    for k in range(3):
        bulk = arr.at[k, pl.ds(0, GROUP - 1)]
        pltpu.make_async_copy(bulk, bulk, send1.at[k]).wait()
        pltpu.make_async_copy(bulk, bulk, send2.at[k]).wait()
        landed = outs[k].at[pl.ds(0, D - PIECE)]
        pltpu.make_async_copy(landed, landed, recv2.at[k]).wait()
        mine = outs[k].at[pl.ds(pl.multiple_of(e * PIECE, PIECE), PIECE)]
        pltpu.make_async_copy(arr.at[k, e], mine, self2_sem.at[k]).wait()
    sent_meta = agm.at[pl.ds(0, ZN - 1)]
    pltpu.make_async_copy(sent_meta, sent_meta, meta_send).wait()
    for p in range(HALF):
        bulk = pbuf.at[p, BULK]
        pltpu.make_async_copy(bulk, bulk, plane_send.at[p]).wait()
        bulk = yret.at[p, BULK]
        pltpu.make_async_copy(bulk, bulk, ret_send.at[p]).wait()
        exchange(prow, orow, p, x_send, x_recv).wait_send()
        exchange(yoth, yin, p, y_send, y_recv).wait_send()


def communicate(partner, ffn_in, mixed_rows, meta, weights):
    bf16, f32 = jnp.bfloat16, jnp.float32
    dma = pltpu.SemaphoreType.DMA
    vmem = pl.BlockSpec(memory_space=pltpu.VMEM)
    anyspace = pl.BlockSpec(memory_space=pl.ANY)
    moved = jax.ShapeDtypeStruct((D, FLOC), bf16)
    return pl.pallas_call(
        kernel,
        out_shape=(jax.ShapeDtypeStruct((TOK, D), bf16), moved, moved, moved),
        in_specs=[pl.BlockSpec(memory_space=pltpu.SMEM), vmem, vmem, vmem] + [anyspace] * 9,
        out_specs=(vmem, anyspace, anyspace, anyspace),
        scratch_shapes=[
            pltpu.VMEM((9, D, FLOC), bf16),
            pltpu.VMEM((3, D, FLOC), bf16),
            pltpu.VMEM((GROUP, PIECE, FLOC), bf16),
            pltpu.VMEM((GROUP, PIECE, FLOC), bf16),
            pltpu.VMEM((GROUP, PIECE, FLOC), bf16),
            pltpu.VMEM((3, GROUP, PIECE, FLOC), bf16),
            pltpu.VMEM((ZN, TOK, D), bf16),
            pltpu.VMEM((ZN, 8, TOK), f32),
            pltpu.VMEM((HALF, ROWS, D), bf16),
            pltpu.VMEM((HALF, ROWS, D), bf16),
            pltpu.VMEM((HALF, ROWS, D), bf16),
            pltpu.VMEM((HALF, ROWS, D), f32),
            pltpu.VMEM((HALF, ROWS, D), bf16),
            pltpu.VMEM((HALF, ROWS, D), bf16),
            pltpu.VMEM((HALF, ROWS, D), bf16),
            pltpu.VMEM((HALF, ROWS, D), bf16),
            pltpu.VMEM((ZN, TOK, D), f32),
            pltpu.VMEM((2, HALF, TOK, D), bf16),
            pltpu.VMEM((2, HALF, TOK, D), bf16),
            dma((9,)),
            dma((3,)),
            dma((3,)),
            dma((3,)),
            dma((3,)),
            dma((3,)),
            dma((3,)),
            dma((2, HALF)),
            dma((2, HALF)),
            dma,
            dma,
            dma((HALF,)),
            dma((HALF,)),
            dma((HALF,)),
            dma((HALF,)),
            dma((HALF,)),
            dma((HALF,)),
            dma((HALF,)),
            dma((HALF,)),
            dma((HALF,)),
            dma((HALF,)),
            dma((2, HALF)),
            dma((2, HALF)),
        ],
        compiler_params=pltpu.CompilerParams(
            collective_id=0, has_side_effects=True, vmem_limit_bytes=64 * 1024 * 1024 - 65536
        ),
    )(partner, ffn_in, mixed_rows, meta, *weights)


def shards(
    frames,
    lengths,
    expert_ids,
    capacity,
    resident,
    partner,
    conv_gain,
    conv_kernel,
    conv_bias,
    ffn_gain,
    router,
    gate_weight,
    up_weight,
    down_weight,
    gate_mean_grad,
    gate_mean_square,
    up_mean_grad,
    up_mean_square,
    down_mean_grad,
    down_mean_square,
):
    devices = lax.axis_size("expert")
    position = lax.axis_index("expert")
    frame_count = frames.shape[0]
    margin = (K - 1) // 2
    span_total = devices * frame_count

    start_pos = position * frame_count
    seq_length = lengths[0]
    offsets = start_pos + jnp.arange(frame_count, dtype=jnp.int32)
    live_rows = (offsets < seq_length).astype(jnp.float32)[:, None]
    inputs_f = frames.astype(jnp.float32)
    normed = (layer_norm(inputs_f, conv_gain) * live_rows).astype(jnp.bfloat16)
    padded = extended(normed, (("expert", 0),), margin)
    wide_pos = start_pos - margin + jnp.arange(frame_count + 2 * margin, dtype=jnp.int32)
    same_utterance = ((wide_pos >= 0) & (wide_pos < span_total)).astype(jnp.float32)[:, None]
    widened = padded.astype(jnp.float32) * same_utterance
    conv_sum = jnp.zeros((frame_count, frames.shape[1]), jnp.float32)
    for tap_index in range(K):
        conv_sum = conv_sum + conv_kernel[tap_index] * widened[tap_index : tap_index + frame_count]
    mixed_rows = (inputs_f + live_rows * jax.nn.silu(conv_sum + conv_bias)).astype(jnp.bfloat16)
    ffn_in = layer_norm(mixed_rows.astype(jnp.float32), ffn_gain).astype(jnp.bfloat16)
    logits = jnp.dot(ffn_in, router, preferred_element_type=jnp.float32)
    expert_iota = jnp.arange(router.shape[1], dtype=jnp.int32)
    picked = expert_ids[:, :, None] == expert_iota[None, None, :]
    chosen = jnp.sum(jnp.where(picked, logits[:, None, :], 0.0), axis=-1)
    scores = jax.nn.sigmoid(chosen)
    gate_values = (scores / jnp.sum(scores, axis=-1, keepdims=True)).astype(jnp.bfloat16)
    old_slot = jnp.sum(
        jnp.where(resident[None, :] == expert_iota[:, None], expert_iota[None, :], 0), axis=1
    )
    place = (old_slot % ZL) * (XY * SLOTS) + (old_slot // ZL) * SLOTS
    flat_ids = expert_ids.reshape(-1)
    onehot = (flat_ids[:, None] == expert_iota[None, :]).astype(jnp.int32)
    earlier = jnp.cumsum(onehot, axis=0) - onehot
    rank_in_block = jnp.sum(earlier * onehot, axis=1)
    slot_limit = jnp.sum(onehot * capacity[None, :], axis=1)
    dest = jnp.sum(onehot * place[None, :], axis=1)
    code = jnp.where(rank_in_block < slot_limit, dest + rank_in_block, -1).reshape(frame_count, 2)
    meta = jnp.concatenate(
        [
            code.astype(jnp.float32).T,
            gate_values.astype(jnp.float32).T,
            jnp.zeros((4, frame_count), jnp.float32),
        ],
        axis=0,
    )
    block_out, fresh_gate, fresh_up, fresh_down = communicate(
        partner,
        ffn_in,
        mixed_rows,
        meta,
        (
            gate_weight[0], gate_mean_grad[0], gate_mean_square[0],
            up_weight[0], up_mean_grad[0], up_mean_square[0],
            down_weight[0], down_mean_grad[0], down_mean_square[0],
        ),
    )
    return (block_out, fresh_gate[None], fresh_up[None], fresh_down[None])


def solution(mesh):
    placed = (
        P(("dp", "expert"), None),
        P("dp"),
        P(("dp", "expert"), None),
        P(),
        P(),
        P(),
        P(),
        P(),
        P(),
        P(),
        P(),
        P("expert", None, "dp"),
        P("expert", None, "dp"),
        P("expert", None, "dp"),
        P("expert", None, "dp"),
        P("expert", None, "dp"),
        P("expert", None, "dp"),
        P("expert", None, "dp"),
        P("expert", None, "dp"),
        P("expert", None, "dp"),
    )
    return jax.shard_map(
        shards,
        mesh=mesh,
        in_specs=placed,
        out_specs=(
            P(("dp", "expert"), None),
            P("expert", None, "dp"),
            P("expert", None, "dp"),
            P("expert", None, "dp"),
        ),
        check_vma=False,
    )
```

```python
import functools

import jax
import jax.numpy as jnp
from jax import lax
from jax.experimental import pallas as pl
from jax.experimental.pallas import tpu as pltpu
from jax.sharding import PartitionSpec as P

D = 1024
FF = 2048
K = 31


LEARNING_RATE = 0.1
ADAM_EPSILON = 1e-08
NORM_EPSILON = 1e-05

MESH = pl.DeviceIdType.MESH
XY = 16
ZL = 4
ZN = 8
HALF = ZN // 2
GROUP = XY * ZL
SLOTS = 8
TOK = 128
FLOC = 512
ROWS = XY * 2 * SLOTS
SIDE = GROUP // 2
WIDE = 48
NARROW = 16
CHUNKS = 6
CCOL = FLOC // 2
MARGIN = (K - 1) // 2
EDGE = 16
TILE = 32
CAPS = (16, 20, SIDE)


def layer_norm(values, gain_row):
    centred = values - jnp.mean(values, axis=-1, keepdims=True)
    variance = jnp.mean(centred * centred, axis=-1, keepdims=True)
    return centred * lax.rsqrt(variance + NORM_EPSILON) * gain_row


def refresh(weight, first_moment, second_moment):
    step_size = (
        LEARNING_RATE
        * first_moment.astype(jnp.float32)
        / (jnp.sqrt(second_moment.astype(jnp.float32)) + ADAM_EPSILON)
    )
    return (weight.astype(jnp.float32) - step_size).astype(jnp.bfloat16)


def silu(value):
    return value / (1.0 + jnp.exp(-value))


def kernel(
    cap,
    send_list_ref,
    source_ref,
    length_ref,
    frames_ref,
    ids_ref,
    table_ref,
    conv_gain_ref,
    taps_ref,
    bias_ref,
    ffn_gain_ref,
    router_ref,
    gw, gm, gs, uw, um, us, dw, dm, ds,
    out_ref,
    fg_ref,
    fu_ref,
    fd_ref,
    win,
    fresh,
    wide,
    normed,
    halo,
    mixed,
    meta_ref,
    got0, got1, got2, got3, got4, got5,
    cs0, cs1, cs2, cs3, cs4, cs5,
    cr0, cr1, cr2, cr3, cr4, cr5,
    arr,
    agx,
    agm,
    pbuf,
    xrow,
    yown,
    yoth,
    yin,
    yret,
    rret,
    part,
    rs_out,
    rs_in,
    halo_send,
    halo_recv,
    load_sem,
    self_sem,
    self2_sem,
    send1,
    recv1,
    sendx,
    recvx,
    send2,
    recv2,
    ring_send,
    ring_recv,
    meta_send,
    meta_recv,
    plane_send,
    plane_recv,
    plane_self,
    x_send,
    x_recv,
    y_send,
    y_recv,
    ret_send,
    ret_recv,
    ret_self,
    rs_send,
    rs_recv,
):
    a = lax.axis_index("dp")
    e = lax.axis_index("expert")
    core = a % 2
    zlo = e % ZL
    xy = e // ZL
    z = (a // 2) * ZL + zlo
    side = zlo // 2
    inner = ((zlo + 1) // 2) % 2
    local = xy * 2 + zlo % 2
    wide_of = 1 + side
    narrow_of = 3 * side

    def line(position):
        return ((position // ZL) * 2 + core, xy * ZL + position % ZL)

    def plane(spot):
        return (a, spot * ZL + zlo)

    partner_core = ((a // 2) * 2 + 1 - core, e)

    barrier = pltpu.get_barrier_semaphore()

    def greet_group(i, _):
        pl.semaphore_signal(barrier, inc=1, device_id=(a, (e + i) % GROUP), device_id_type=MESH)
        return _

    lax.fori_loop(1, GROUP, greet_group, 0)

    def greet_line(i, _):
        far = (1 - a // 2) * ZL + i
        pl.semaphore_signal(barrier, inc=1, device_id=line(far), device_id_type=MESH)
        return _

    lax.fori_loop(0, ZL, greet_line, 0)
    pl.semaphore_signal(barrier, inc=1, device_id=partner_core, device_id_type=MESH)

    sources = ((gw, gm, gs), (uw, um, us), (dw, dm, ds))

    def load(c, i):
        columns = pl.ds((c % 2) * CCOL, CCOL)
        return pltpu.make_async_copy(
            sources[c // 2][i].at[:, columns], win.at[c % 3, i], load_sem.at[c % 3, i]
        )

    for c in range(3):
        for i in range(3):
            load(c, i).start()

    length = length_ref[0]

    def first_norm(i, _):
        rows = pl.ds(pl.multiple_of(i * TILE, TILE), TILE)
        offset = e * TOK + i * TILE + lax.broadcasted_iota(jnp.int32, (TILE, 1), 0)
        live = jnp.where(offset < length, 1.0, 0.0)
        value = layer_norm(frames_ref[rows, :].astype(jnp.float32), conv_gain_ref[...]) * live
        value = value.astype(jnp.bfloat16)
        normed[rows, :] = value
        wide[pl.ds(pl.multiple_of(EDGE + i * TILE, EDGE), TILE), :] = value.astype(jnp.float32)
        return _

    lax.fori_loop(0, TOK // TILE, first_norm, 0)
    pl.semaphore_wait(barrier, GROUP + ZL)

    def edge(way):
        start = TOK - EDGE if way == 0 else 0
        neighbour = (e + 1) % GROUP if way == 0 else (e - 1 + GROUP) % GROUP
        return pltpu.make_async_remote_copy(
            src_ref=normed.at[pl.ds(start, EDGE)],
            dst_ref=halo.at[way],
            send_sem=halo_send.at[way],
            recv_sem=halo_recv.at[way],
            device_id=(a, neighbour),
            device_id_type=MESH,
        )

    for way in range(2):
        edge(way).start()

    def ring(step, way):
        if way == 0:
            block = (z - step + 1 + ZN) % ZN
            target = line((z + 1) % ZN)
        else:
            block = (z + step - 1) % ZN
            target = line((z - 1 + ZN) % ZN)
        if step == HALF:
            view = agx.at[block, pl.ds(way * (TOK // 2), TOK // 2)]
        else:
            view = agx.at[block]
        return pltpu.make_async_remote_copy(
            src_ref=view,
            dst_ref=view,
            send_sem=ring_send.at[way, step - 1],
            recv_sem=ring_recv.at[way, step - 1],
            device_id=target,
            device_id_type=MESH,
        )

    def ring_arrival(step, way):
        if way == 0:
            block = (z - step + ZN) % ZN
        else:
            block = (z + step) % ZN
        if step == HALF:
            view = agx.at[block, pl.ds(way * (TOK // 2), TOK // 2)]
        else:
            view = agx.at[block]
        pltpu.make_async_copy(view, view, ring_recv.at[way, step - 1]).wait()

    def meta_copy(i):
        return pltpu.make_async_remote_copy(
            src_ref=meta_ref,
            dst_ref=agm.at[z],
            send_sem=meta_send,
            recv_sem=meta_recv,
            device_id=line((z + i) % ZN),
            device_id_type=MESH,
        )

    def send_meta(i, _):
        meta_copy(i).start()
        return _

    gots = (got0, got1, got2, got3, got4, got5)
    crosses_out = (cs0, cs1, cs2, cs3, cs4, cs5)
    crosses_in = (cr0, cr1, cr2, cr3, cr4, cr5)
    outs = (fg_ref, fu_ref, fd_ref)

    def refresh_chunk(k):
        for i in range(3):
            load(k, i).wait()
        slot = k % 3

        def tile(i, _):
            rows = pl.ds(pl.multiple_of(i * 64, 64), 64)
            fresh[k // 2, rows, pl.ds((k % 2) * CCOL, CCOL)] = refresh(
                win[slot, 0, rows, :], win[slot, 1, rows, :], win[slot, 2, rows, :]
            )
            return _

        lax.fori_loop(0, D // 64, tile, 0)
        if k + 3 < CHUNKS:
            for i in range(3):
                load(k + 3, i).start()

    def fresh_rows(k, rows):
        return fresh.at[k // 2, rows, pl.ds((k % 2) * CCOL, CCOL)]

    def out_rows(k, rows):
        return outs[k // 2].at[rows, pl.ds((k % 2) * CCOL, CCOL)]

    def wide_rows(spot):
        return pl.ds(pl.multiple_of(spot * WIDE, NARROW), WIDE)

    def narrow_rows(spot):
        return pl.ds(pl.multiple_of(XY * WIDE + spot * NARROW, NARROW), NARROW)

    TALL = pl.ds(0, D - WIDE)
    TALLER = pl.ds(0, D - NARROW)
    PART = pl.ds(0, NARROW)
    MOST = pl.ds(0, SIDE - 1)

    def wait_bytes(view, sem):
        pltpu.make_async_copy(view, view, sem).wait()

    def scatter_chunk(k):
        got = gots[k]

        def to_wide(spot):
            return pltpu.make_async_remote_copy(
                src_ref=fresh_rows(k, wide_rows(spot)),
                dst_ref=got.at[local],
                send_sem=send1.at[k],
                recv_sem=recv1.at[k],
                device_id=(a, spot * ZL + wide_of),
                device_id_type=MESH,
            )

        def to_narrow(spot):
            return pltpu.make_async_remote_copy(
                src_ref=fresh_rows(k, narrow_rows(spot)),
                dst_ref=got.at[local, PART],
                send_sem=send1.at[k],
                recv_sem=recv1.at[k],
                device_id=(a, spot * ZL + narrow_of),
                device_id_type=MESH,
            )

        @pl.when(inner == 1)
        def _inner():
            pltpu.make_async_copy(fresh_rows(k, wide_rows(xy)), got.at[local], self_sem.at[k]).start()
            to_narrow(xy).start()

        @pl.when(inner == 0)
        def _outer():
            pltpu.make_async_copy(fresh_rows(k, narrow_rows(xy)), got.at[local, PART], self_sem.at[k]).start()
            to_wide(xy).start()

        def send(i, _):
            spot = ((xy // 4 + i // 4) % 4) * 4 + (xy + i) % 4
            to_wide(spot).start()
            to_narrow(spot).start()
            return _

        lax.fori_loop(1, XY, send, 0)

    def cross_copy(k, narrow):
        src, dst = crosses_out[k], crosses_in[k]
        return pltpu.make_async_remote_copy(
            src_ref=src.at[:, PART] if narrow else src,
            dst_ref=dst.at[:, PART] if narrow else dst,
            send_sem=sendx.at[k],
            recv_sem=recvx.at[k],
            device_id=(a, xy * ZL + ZL - 1 - zlo),
            device_id_type=MESH,
        )

    def cross_chunk(k):
        got, out = gots[k], crosses_out[k]

        @pl.when(inner == 1)
        def _inner():
            wait_bytes(got.at[MOST], recv1.at[k])
            pltpu.make_async_copy(fresh_rows(k, wide_rows(xy)), got.at[local], self_sem.at[k]).wait()

        @pl.when(inner == 0)
        def _outer():
            wait_bytes(got.at[MOST, PART], recv1.at[k])
            pltpu.make_async_copy(fresh_rows(k, narrow_rows(xy)), got.at[local, PART], self_sem.at[k]).wait()

        def pick(i, _):
            out[i] = got[send_list_ref[i]]
            return _

        lax.fori_loop(0, cap, pick, 0)

        @pl.when(inner == 1)
        def _send_inner():
            cross_copy(k, False).start()

        @pl.when(inner == 0)
        def _send_outer():
            cross_copy(k, True).start()

    def regroup_chunk(k):
        got, crossed = gots[k], crosses_in[k]

        @pl.when(inner == 1)
        def _inner():
            cross_copy(k, False).wait_recv()

        @pl.when(inner == 0)
        def _outer():
            cross_copy(k, True).wait_recv()

        def pick(i, _):
            index = source_ref[i]
            near = got[jnp.minimum(index, SIDE - 1)]
            far = crossed[jnp.maximum(index - SIDE, 0)]
            arr[k, i] = jnp.where(index < SIDE, near, far)
            return _

        lax.fori_loop(0, SIDE, pick, 0)

        def deliver(rows, part):
            def view(i):
                return arr.at[k, i, part] if part is not None else arr.at[k, i]

            pltpu.make_async_copy(view(local), out_rows(k, rows), self2_sem.at[k]).start()

            def send(i, _):
                spot = ((xy // 4 + i // 8) % 4) * 4 + (xy + i // 2) % 4
                end = (zlo + i) % 2
                pltpu.make_async_remote_copy(
                    src_ref=view(spot * 2 + end),
                    dst_ref=out_rows(k, rows),
                    send_sem=send2.at[k],
                    recv_sem=recv2.at[k],
                    device_id=(a, spot * ZL + side * 2 + end),
                    device_id_type=MESH,
                ).start()
                return _

            lax.fori_loop(1, SIDE, send, 0)

        @pl.when(inner == 1)
        def _deliver_inner():
            deliver(wide_rows(xy), None)

        @pl.when(inner == 0)
        def _deliver_outer():
            deliver(narrow_rows(xy), PART)

    def frame_module():
        for way in range(2):
            edge(way).wait_recv()
        has_left = jnp.where(e > 0, 1.0, 0.0)
        has_right = jnp.where(e < GROUP - 1, 1.0, 0.0)
        wide[pl.ds(0, EDGE), :] = halo[0].astype(jnp.float32) * has_left
        wide[pl.ds(EDGE + TOK, EDGE), :] = halo[1].astype(jnp.float32) * has_right
        offset = e * TOK + lax.broadcasted_iota(jnp.int32, (TOK, 1), 0)
        live = jnp.where(offset < length, 1.0, 0.0)

        def columns_step(i, _):
            columns = pl.ds(pl.multiple_of(i * 128, 128), 128)
            total = jnp.zeros((TOK, 128), jnp.float32)
            for tap in range(K):
                total = total + taps_ref[pl.ds(tap, 1), columns] * wide[pl.ds(EDGE - MARGIN + tap, TOK), columns]
            total = total + bias_ref[:, columns]
            mixed[:, columns] = (
                frames_ref[:, columns].astype(jnp.float32) + live * silu(total)
            ).astype(jnp.bfloat16)
            return _

        lax.fori_loop(0, D // 128, columns_step, 0)

        def second_norm(i, _):
            rows = pl.ds(pl.multiple_of(i * TILE, TILE), TILE)
            value = layer_norm(mixed[rows, :].astype(jnp.float32), ffn_gain_ref[...])
            agx[z, rows, :] = value.astype(jnp.bfloat16)
            return _

        lax.fori_loop(0, TOK // TILE, second_norm, 0)
        for way in range(2):
            ring(1, way).start()

        logits = lax.dot_general(
            router_ref[...], agx[z], (((0,), (1,)), ((), ())), preferred_element_type=jnp.float32
        )
        experts_iota = lax.broadcasted_iota(jnp.int32, (GROUP, TOK), 0)
        picked = [experts_iota == ids_ref[pl.ds(k, 1), :] for k in range(2)]
        named = jnp.where(picked[0] | picked[1], 1.0, 0.0).astype(jnp.bfloat16)
        before = lax.broadcasted_iota(jnp.int32, (TOK, TOK), 0) < lax.broadcasted_iota(jnp.int32, (TOK, TOK), 1)
        earlier = jnp.dot(
            named, jnp.where(before, 1.0, 0.0).astype(jnp.bfloat16), preferred_element_type=jnp.float32
        )
        limit, place = table_ref[:, 0:1], table_ref[:, 1:2]

        def of(k, values):
            return jnp.sum(jnp.where(picked[k], values, 0.0), axis=0, keepdims=True)

        scores = [1.0 / (1.0 + jnp.exp(-of(k, logits))) for k in range(2)]
        both = scores[0] + scores[1]
        for k in range(2):
            rank = of(k, earlier)
            meta_ref[pl.ds(k, 1), :] = jnp.where(rank < of(k, limit), of(k, place) + rank, -1.0)
            gate = (scores[k] / both).astype(jnp.bfloat16)
            meta_ref[pl.ds(2 + k, 1), :] = gate.astype(jnp.float32)
        meta_ref[pl.ds(4, 4), :] = jnp.zeros((4, TOK), jnp.float32)
        agm[z] = meta_ref[...]
        lax.fori_loop(1, ZN, send_meta, 0)

    def pair_blocks(p):
        first = (z - (p + 1) % HALF + ZN) % ZN
        second = (z + 1 + p) % ZN
        return first, second

    def choices(p):
        first, second = pair_blocks(p)
        ma, mb = agm[first], agm[second]
        row = lax.broadcasted_iota(jnp.int32, (ROWS, 1), 0)
        column = lax.broadcasted_iota(jnp.int32, (1, 2 * TOK), 1)
        code = (zlo * (XY * SLOTS) + (row // (2 * SLOTS)) * SLOTS + row % SLOTS).astype(jnp.float32)
        same = (row // SLOTS) % 2 == column // TOK
        both = jnp.concatenate([ma, mb], axis=1)
        hit0 = (both[0:1] == code) & same
        hit1 = (both[1:2] == code) & same
        return hit0, hit1, both

    def dispatch(p):
        first, second = pair_blocks(p)
        hit0, hit1, _ = choices(p)
        select = jnp.where(hit0 | hit1, 1.0, 0.0).astype(jnp.bfloat16)
        rows = jnp.dot(select[:, :TOK], agx[first], preferred_element_type=jnp.float32)
        rows = rows + jnp.dot(select[:, TOK:], agx[second], preferred_element_type=jnp.float32)
        pbuf[p] = rows.astype(jnp.bfloat16)
        mine = xrow.at[p, pl.ds(pl.multiple_of(xy * 2 * SLOTS, 2 * SLOTS), 2 * SLOTS)]
        pltpu.make_async_copy(
            pbuf.at[p, pl.ds(pl.multiple_of(xy * 2 * SLOTS, 2 * SLOTS), 2 * SLOTS)], mine, plane_self.at[p]
        ).start()

        def send(i, _):
            spot = (xy + i) % XY
            pltpu.make_async_remote_copy(
                src_ref=pbuf.at[p, pl.ds(pl.multiple_of(spot * 2 * SLOTS, 2 * SLOTS), 2 * SLOTS)],
                dst_ref=mine,
                send_sem=plane_send.at[p],
                recv_sem=plane_recv.at[p],
                device_id=plane(spot),
                device_id_type=MESH,
            ).start()
            return _

        lax.fori_loop(1, XY, send, 0)

    BULK = pl.ds(0, ROWS - 2 * SLOTS)
    OWN = pl.ds(pl.multiple_of(xy * 2 * SLOTS, 2 * SLOTS), 2 * SLOTS)

    def begin(k):
        refresh_chunk(k)
        scatter_chunk(k)

    begin(0)
    begin(1)
    frame_module()
    begin(2)
    cross_chunk(0)
    for p in range(HALF):
        for way in range(2):
            ring_arrival(p + 1, way)
        if p + 2 <= HALF:
            for way in range(2):
                ring(p + 2, way).start()
        if p == 0:
            line_meta = agm.at[pl.ds(0, ZN - 1)]
            wait_bytes(line_meta, meta_recv)
        dispatch(p)
        if p < 3:
            begin(p + 3)
            cross_chunk(p + 1)
        if p == 2:
            regroup_chunk(0)
    cross_chunk(4)
    regroup_chunk(1)

    def expert_part(rows):
        gate_pre = jnp.dot(rows, fresh[0], preferred_element_type=jnp.float32) * D ** (-0.5)
        up_pre = jnp.dot(rows, fresh[1], preferred_element_type=jnp.float32) * D ** (-0.5)
        hidden = (silu(gate_pre) * up_pre).astype(jnp.bfloat16)
        return lax.dot_general(
            hidden, fresh[2], (((1,), (1,)), ((), ())), preferred_element_type=jnp.float32
        ) * FF ** (-0.5)

    def rows_copy(p):
        return pltpu.make_async_remote_copy(
            src_ref=xrow.at[p, pl.ds(0, ROWS)],
            dst_ref=xrow.at[p, pl.ds(ROWS, ROWS)],
            send_sem=x_send.at[p],
            recv_sem=x_recv.at[p],
            device_id=partner_core,
            device_id_type=MESH,
        )

    def sums_copy(p):
        return pltpu.make_async_remote_copy(
            src_ref=yoth.at[p],
            dst_ref=yin.at[p],
            send_sem=y_send.at[p],
            recv_sem=y_recv.at[p],
            device_id=partner_core,
            device_id_type=MESH,
        )

    def pass_rows(p):
        wait_bytes(xrow.at[p, BULK], plane_recv.at[p])
        pltpu.make_async_copy(pbuf.at[p, OWN], xrow.at[p, OWN], plane_self.at[p]).wait()
        rows_copy(p).start()

    def settle(p):
        sums_copy(p).wait_recv()
        yret[p] = (yown[p % 2] + yin[p].astype(jnp.float32)).astype(jnp.bfloat16)
        pltpu.make_async_copy(yret.at[p, OWN], rret.at[p, OWN], ret_self.at[p]).start()

        def send(i, _):
            spot = (xy + i) % XY
            pltpu.make_async_remote_copy(
                src_ref=yret.at[p, pl.ds(pl.multiple_of(spot * 2 * SLOTS, 2 * SLOTS), 2 * SLOTS)],
                dst_ref=rret.at[p, OWN],
                send_sem=ret_send.at[p],
                recv_sem=ret_recv.at[p],
                device_id=plane(spot),
                device_id_type=MESH,
            ).start()
            return _

        lax.fori_loop(1, XY, send, 0)

    pass_rows(0)
    for p in range(HALF):
        if p + 1 < HALF:
            pass_rows(p + 1)
        rows_copy(p).wait_recv()
        result = expert_part(xrow[p])
        yown[p % 2] = result[:ROWS]
        yoth[p] = result[ROWS:].astype(jnp.bfloat16)
        sums_copy(p).start()
        if p > 0:
            settle(p - 1)
        if p == 1:
            cross_chunk(5)
    settle(HALF - 1)
    regroup_chunk(2)

    def combine(p, _):
        bulk = rret.at[p, BULK]
        pltpu.make_async_copy(bulk, bulk, ret_recv.at[p]).wait()
        pltpu.make_async_copy(yret.at[p, OWN], rret.at[p, OWN], ret_self.at[p]).wait()
        first, second = pair_blocks(p)
        hit0, hit1, both = choices(p)
        weights = jnp.where(hit0, both[2:3], 0.0) + jnp.where(hit1, both[3:4], 0.0)
        weights = weights.T.astype(jnp.bfloat16)
        total = jnp.dot(weights, rret[p], preferred_element_type=jnp.float32)
        part[first] = total[:TOK]
        part[second] = total[TOK:]
        return _

    lax.fori_loop(0, HALF, combine, 0)

    def rs_view(ref, step, way):
        if step == 1:
            return ref.at[way, step - 1, pl.ds(way * (TOK // 2), TOK // 2)]
        return ref.at[way, step - 1]

    def rs(step, way):
        target = line((z + 1) % ZN) if way == 0 else line((z - 1 + ZN) % ZN)
        return pltpu.make_async_remote_copy(
            src_ref=rs_view(rs_out, step, way),
            dst_ref=rs_view(rs_in, step, way),
            send_sem=rs_send.at[way, step - 1],
            recv_sem=rs_recv.at[way, step - 1],
            device_id=target,
            device_id_type=MESH,
        )

    for step in range(1, HALF + 1):
        for way in range(2):
            distance = HALF + 1 - step
            owner = (z + distance) % ZN if way == 0 else (z - distance + ZN) % ZN
            half = pl.ds(way * (TOK // 2), TOK // 2)
            other_half = pl.ds((1 - way) * (TOK // 2), TOK // 2)
            if step > 1:
                rs(step - 1, way).wait_recv()
            if step == 1:
                rs_out[way, 0, half, :] = part[owner, half, :].astype(jnp.bfloat16)
            elif step == 2:
                rs_out[way, 1, half, :] = (
                    part[owner, half, :] + rs_in[way, 0, half, :].astype(jnp.float32)
                ).astype(jnp.bfloat16)
                rs_out[way, 1, other_half, :] = part[owner, other_half, :].astype(jnp.bfloat16)
            else:
                rs_out[way, step - 1] = (
                    part[owner] + rs_in[way, step - 2].astype(jnp.float32)
                ).astype(jnp.bfloat16)
            rs(step, way).start()
        if step == 1:
            regroup_chunk(3)
        if step == 3:
            regroup_chunk(4)
        if step == 4:
            regroup_chunk(5)
    for way in range(2):
        rs(HALF, way).wait_recv()
    moe = (
        part[z]
        + rs_in[0, HALF - 1].astype(jnp.float32)
        + rs_in[1, HALF - 1].astype(jnp.float32)
    )
    out_ref[...] = (mixed[...].astype(jnp.float32) + 0.5 * moe).astype(jnp.bfloat16)

    for way in range(2):
        for step in range(1, HALF + 1):
            ring(step, way).wait_send()
            rs(step, way).wait_send()
    for way in range(2):
        edge(way).wait_send()
    for k in range(CHUNKS):

        @pl.when(inner == 1)
        def _inner():
            wait_bytes(fresh_rows(k, pl.ds(0, (XY - 1) * WIDE + XY * NARROW)), send1.at[k])
            cross_copy(k, False).wait_send()
            wait_bytes(arr.at[k, MOST], send2.at[k])
            wait_bytes(out_rows(k, TALL), recv2.at[k])
            pltpu.make_async_copy(arr.at[k, local], out_rows(k, wide_rows(xy)), self2_sem.at[k]).wait()

        @pl.when(inner == 0)
        def _outer():
            wait_bytes(fresh_rows(k, pl.ds(0, XY * WIDE + (XY - 1) * NARROW)), send1.at[k])
            cross_copy(k, True).wait_send()
            wait_bytes(arr.at[k, MOST, PART], send2.at[k])
            wait_bytes(out_rows(k, TALLER), recv2.at[k])
            pltpu.make_async_copy(arr.at[k, local, PART], out_rows(k, narrow_rows(xy)), self2_sem.at[k]).wait()

    sent_meta = agm.at[pl.ds(0, ZN - 1)]
    pltpu.make_async_copy(sent_meta, sent_meta, meta_send).wait()
    for p in range(HALF):
        bulk = pbuf.at[p, BULK]
        pltpu.make_async_copy(bulk, bulk, plane_send.at[p]).wait()
        bulk = yret.at[p, BULK]
        pltpu.make_async_copy(bulk, bulk, ret_send.at[p]).wait()
        rows_copy(p).wait_send()
        sums_copy(p).wait_send()


def communicate(cap, ident, send_list, source, length, small, weights):
    bf16, f32 = jnp.bfloat16, jnp.float32
    dma = pltpu.SemaphoreType.DMA
    vmem = pl.BlockSpec(memory_space=pltpu.VMEM)
    anyspace = pl.BlockSpec(memory_space=pl.ANY)
    moved = jax.ShapeDtypeStruct((D, FLOC), bf16)
    return pl.pallas_call(
        functools.partial(kernel, cap),
        out_shape=(jax.ShapeDtypeStruct((TOK, D), bf16), moved, moved, moved),
        in_specs=[pl.BlockSpec(memory_space=pltpu.SMEM)] * 3 + [vmem] * 8 + [anyspace] * 9,
        out_specs=(vmem, anyspace, anyspace, anyspace),
        scratch_shapes=[
            pltpu.VMEM((3, 3, D, CCOL), bf16),
            pltpu.VMEM((3, D, FLOC), bf16),
            pltpu.VMEM((TOK + 2 * EDGE, D), f32),
            pltpu.VMEM((TOK, D), bf16),
            pltpu.VMEM((2, EDGE, D), bf16),
            pltpu.VMEM((TOK, D), bf16),
            pltpu.VMEM((8, TOK), f32),
        ]
        + [pltpu.VMEM((SIDE, WIDE, CCOL), bf16)] * CHUNKS
        + [pltpu.VMEM((cap, WIDE, CCOL), bf16)] * (2 * CHUNKS)
        + [
            pltpu.VMEM((CHUNKS, SIDE, WIDE, CCOL), bf16),
            pltpu.VMEM((ZN, TOK, D), bf16),
            pltpu.VMEM((ZN, 8, TOK), f32),
            pltpu.VMEM((HALF, ROWS, D), bf16),
            pltpu.VMEM((HALF, 2 * ROWS, D), bf16),
            pltpu.VMEM((2, ROWS, D), f32),
            pltpu.VMEM((HALF, ROWS, D), bf16),
            pltpu.VMEM((HALF, ROWS, D), bf16),
            pltpu.VMEM((HALF, ROWS, D), bf16),
            pltpu.VMEM((HALF, ROWS, D), bf16),
            pltpu.VMEM((ZN, TOK, D), f32),
            pltpu.VMEM((2, HALF, TOK, D), bf16),
            pltpu.VMEM((2, HALF, TOK, D), bf16),
            dma((2,)),
            dma((2,)),
            dma((3, 3)),
            dma((CHUNKS,)),
            dma((CHUNKS,)),
            dma((CHUNKS,)),
            dma((CHUNKS,)),
            dma((CHUNKS,)),
            dma((CHUNKS,)),
            dma((CHUNKS,)),
            dma((CHUNKS,)),
            dma((2, HALF)),
            dma((2, HALF)),
            dma,
            dma,
            dma((HALF,)),
            dma((HALF,)),
            dma((HALF,)),
            dma((HALF,)),
            dma((HALF,)),
            dma((HALF,)),
            dma((HALF,)),
            dma((HALF,)),
            dma((HALF,)),
            dma((HALF,)),
            dma((2, HALF)),
            dma((2, HALF)),
        ],
        compiler_params=pltpu.CompilerParams(
            collective_id=ident, has_side_effects=True, vmem_limit_bytes=64 * 1024 * 1024 - 65536
        ),
    )(send_list, source, length, *small, *weights)


def shards(
    frames,
    lengths,
    expert_ids,
    capacity,
    resident,
    partner,
    conv_gain,
    conv_kernel,
    conv_bias,
    ffn_gain,
    router,
    gate_weight,
    up_weight,
    down_weight,
    gate_mean_grad,
    gate_mean_square,
    up_mean_grad,
    up_mean_square,
    down_mean_grad,
    down_mean_square,
):
    position = lax.axis_index("expert")
    expert_iota = jnp.arange(GROUP, dtype=jnp.int32)
    old_slot = jnp.sum(
        jnp.where(resident[None, :] == expert_iota[:, None], expert_iota[None, :], 0), axis=1
    )
    place = (old_slot % ZL) * (XY * SLOTS) + (old_slot // ZL) * SLOTS
    table = jnp.stack([capacity, place], axis=1).astype(jnp.float32)
    half_of = (expert_iota % ZL) // 2
    local_of = (expert_iota // ZL) * 2 + expert_iota % 2
    same_half = half_of[:, None] == half_of[None, :]
    paired = partner[:, None] == expert_iota[None, :]
    partner_half = jnp.sum(jnp.where(paired, half_of[None, :], 0), axis=1)
    crossing = half_of != partner_half
    ahead = same_half & (local_of[None, :] < local_of[:, None]) & crossing[None, :]
    order = jnp.sum(ahead.astype(jnp.int32), axis=1)
    my_half = (position % ZL) // 2
    mine = half_of == my_half
    send_list = jnp.sum(
        jnp.where(
            (mine & crossing)[None, :] & (order[None, :] == jnp.arange(SIDE, dtype=jnp.int32)[:, None]),
            local_of[None, :],
            0,
        ),
        axis=1,
    )
    source_of = jnp.where(crossing[:, None], SIDE + order[None, :], local_of[None, :])
    source_of = jnp.sum(jnp.where(paired, source_of, 0), axis=1)
    source = jnp.sum(
        jnp.where(
            mine[None, :] & (local_of[None, :] == jnp.arange(SIDE, dtype=jnp.int32)[:, None]),
            source_of[None, :],
            0,
        ),
        axis=1,
    )
    crossings = jnp.sum(crossing.astype(jnp.int32)) // 2
    operands = (
        send_list,
        source,
        lengths,
        (
            frames,
            expert_ids.T,
            table,
            conv_gain[None],
            conv_kernel,
            conv_bias[None],
            ffn_gain[None],
            router,
        ),
        (
            gate_weight[0], gate_mean_grad[0], gate_mean_square[0],
            up_weight[0], up_mean_grad[0], up_mean_square[0],
            down_weight[0], down_mean_grad[0], down_mean_square[0],
        ),
    )
    level = sum((crossings > cap).astype(jnp.int32) for cap in CAPS[:-1])
    block_out, fresh_gate, fresh_up, fresh_down = lax.switch(
        level,
        [
            lambda operands, cap=cap, ident=ident: communicate(cap, ident, *operands)
            for ident, cap in enumerate(CAPS)
        ],
        operands,
    )
    return (block_out, fresh_gate[None], fresh_up[None], fresh_down[None])


def solution(mesh):
    placed = (
        P(("dp", "expert"), None),
        P("dp"),
        P(("dp", "expert"), None),
        P(),
        P(),
        P(),
        P(),
        P(),
        P(),
        P(),
        P(),
        P("expert", None, "dp"),
        P("expert", None, "dp"),
        P("expert", None, "dp"),
        P("expert", None, "dp"),
        P("expert", None, "dp"),
        P("expert", None, "dp"),
        P("expert", None, "dp"),
        P("expert", None, "dp"),
        P("expert", None, "dp"),
    )
    return jax.shard_map(
        shards,
        mesh=mesh,
        in_specs=placed,
        out_specs=(
            P(("dp", "expert"), None),
            P("expert", None, "dp"),
            P("expert", None, "dp"),
            P("expert", None, "dp"),
        ),
        check_vma=False,
    )
```

```python
import functools

import jax
import jax.numpy as jnp
from jax import lax
from jax.experimental import pallas as pl
from jax.experimental.pallas import tpu as pltpu
from jax.sharding import PartitionSpec as P

D = 1024
FF = 2048
K = 31


LEARNING_RATE = 0.1
ADAM_EPSILON = 1e-08
NORM_EPSILON = 1e-05

MESH = pl.DeviceIdType.MESH
XY = 16
ZL = 4
ZN = 8
HALF = ZN // 2
GROUP = XY * ZL
SLOTS = 8
TOK = 128
FLOC = 512
ROWS = XY * 2 * SLOTS
SIDE = GROUP // 2
WIDE = 48
NARROW = 16
CHUNKS = 6
CCOL = FLOC // 2
MARGIN = (K - 1) // 2
EDGE = 16
TILE = 32
CAPS = (18, 22, SIDE)


def layer_norm(values, gain_row):
    centred = values - jnp.mean(values, axis=-1, keepdims=True)
    variance = jnp.mean(centred * centred, axis=-1, keepdims=True)
    return centred * lax.rsqrt(variance + NORM_EPSILON) * gain_row


def refresh(weight, first_moment, second_moment):
    step_size = (
        LEARNING_RATE
        * first_moment.astype(jnp.float32)
        / (jnp.sqrt(second_moment.astype(jnp.float32)) + ADAM_EPSILON)
    )
    return (weight.astype(jnp.float32) - step_size).astype(jnp.bfloat16)


def silu(value):
    return value / (1.0 + jnp.exp(-value))


def kernel(
    cap,
    plan_ref,
    length_ref,
    frames_ref,
    ids_ref,
    resident_ref,
    capacity_ref,
    conv_gain_ref,
    taps_ref,
    bias_ref,
    ffn_gain_ref,
    router_ref,
    gw, gm, gs, uw, um, us, dw, dm, ds,
    out_ref,
    fg_ref,
    fu_ref,
    fd_ref,
    win,
    fresh,
    wide,
    normed,
    halo,
    mixed,
    meta_ref,
    got0, got1, got2, got3, got4, got5,
    cs0, cs1, cs2, cs3, cs4, cs5,
    cr0, cr1, cr2, cr3, cr4, cr5,
    arr,
    agx,
    agm,
    pbuf,
    xrow,
    yown,
    yoth,
    yin,
    yret,
    rret,
    part,
    rs_out,
    rs_in,
    halo_send,
    halo_recv,
    load_sem,
    self_sem,
    self2_sem,
    send1,
    recv1,
    sendx,
    recvx,
    send2,
    recv2,
    ring_send,
    ring_recv,
    meta_send,
    meta_recv,
    plane_send,
    plane_recv,
    plane_self,
    x_send,
    x_recv,
    y_send,
    y_recv,
    ret_send,
    ret_recv,
    ret_self,
    rs_send,
    rs_recv,
):
    a = lax.axis_index("dp")
    e = lax.axis_index("expert")
    core = a % 2
    zlo = e % ZL
    xy = e // ZL
    z = (a // 2) * ZL + zlo
    side = zlo // 2
    inner = ((zlo + 1) // 2) % 2
    local = xy * 2 + zlo % 2
    wide_of = 1 + side
    narrow_of = 3 * side

    def line(position):
        return ((position // ZL) * 2 + core, xy * ZL + position % ZL)

    def plane(spot):
        return (a, spot * ZL + zlo)

    partner_core = ((a // 2) * 2 + 1 - core, e)

    barrier = pltpu.get_barrier_semaphore()

    def greet_group(i, _):
        pl.semaphore_signal(barrier, inc=1, device_id=(a, (e + i) % GROUP), device_id_type=MESH)
        return _

    lax.fori_loop(1, GROUP, greet_group, 0)

    def greet_line(i, _):
        far = (1 - a // 2) * ZL + i
        pl.semaphore_signal(barrier, inc=1, device_id=line(far), device_id_type=MESH)
        return _

    lax.fori_loop(0, ZL, greet_line, 0)
    pl.semaphore_signal(barrier, inc=1, device_id=partner_core, device_id_type=MESH)

    sources = ((gw, gm, gs), (uw, um, us), (dw, dm, ds))

    def load(c, i):
        columns = pl.ds((c % 2) * CCOL, CCOL)
        return pltpu.make_async_copy(
            sources[c // 2][i].at[:, columns], win.at[c % 3, i], load_sem.at[c % 3, i]
        )

    for c in range(3):
        for i in range(3):
            load(c, i).start()

    def refresh_chunk(k):
        for i in range(3):
            load(k, i).wait()
        slot = k % 3

        def tile(i, _):
            rows = pl.ds(pl.multiple_of(i * 64, 64), 64)
            fresh[k // 2, rows, pl.ds((k % 2) * CCOL, CCOL)] = refresh(
                win[slot, 0, rows, :], win[slot, 1, rows, :], win[slot, 2, rows, :]
            )
            return _

        lax.fori_loop(0, D // 64, tile, 0)
        if k + 3 < CHUNKS:
            for i in range(3):
                load(k + 3, i).start()

    refresh_chunk(0)

    length = length_ref[0]

    def first_norm(i, _):
        rows = pl.ds(pl.multiple_of(i * TILE, TILE), TILE)
        offset = e * TOK + i * TILE + lax.broadcasted_iota(jnp.int32, (TILE, 1), 0)
        live = jnp.where(offset < length, 1.0, 0.0)
        value = layer_norm(frames_ref[rows, :].astype(jnp.float32), conv_gain_ref[...]) * live
        value = value.astype(jnp.bfloat16)
        normed[rows, :] = value
        wide[pl.ds(pl.multiple_of(EDGE + i * TILE, EDGE), TILE), :] = value.astype(jnp.float32)
        return _

    lax.fori_loop(0, TOK // TILE, first_norm, 0)
    pl.semaphore_wait(barrier, GROUP + ZL)

    def edge(way):
        start = TOK - EDGE if way == 0 else 0
        neighbour = (e + 1) % GROUP if way == 0 else (e - 1 + GROUP) % GROUP
        return pltpu.make_async_remote_copy(
            src_ref=normed.at[pl.ds(start, EDGE)],
            dst_ref=halo.at[way],
            send_sem=halo_send.at[way],
            recv_sem=halo_recv.at[way],
            device_id=(a, neighbour),
            device_id_type=MESH,
        )

    for way in range(2):
        edge(way).start()

    def ring(step, way):
        if way == 0:
            block = (z - step + 1 + ZN) % ZN
            target = line((z + 1) % ZN)
        else:
            block = (z + step - 1) % ZN
            target = line((z - 1 + ZN) % ZN)
        if step == HALF:
            view = agx.at[block, pl.ds(way * (TOK // 2), TOK // 2)]
        else:
            view = agx.at[block]
        return pltpu.make_async_remote_copy(
            src_ref=view,
            dst_ref=view,
            send_sem=ring_send.at[way, step - 1],
            recv_sem=ring_recv.at[way, step - 1],
            device_id=target,
            device_id_type=MESH,
        )

    def ring_arrival(step, way):
        if way == 0:
            block = (z - step + ZN) % ZN
        else:
            block = (z + step) % ZN
        if step == HALF:
            view = agx.at[block, pl.ds(way * (TOK // 2), TOK // 2)]
        else:
            view = agx.at[block]
        pltpu.make_async_copy(view, view, ring_recv.at[way, step - 1]).wait()

    def meta_copy(i):
        return pltpu.make_async_remote_copy(
            src_ref=meta_ref,
            dst_ref=agm.at[z],
            send_sem=meta_send,
            recv_sem=meta_recv,
            device_id=line((z + i) % ZN),
            device_id_type=MESH,
        )

    def send_meta(i, _):
        meta_copy(i).start()
        return _

    gots = (got0, got1, got2, got3, got4, got5)
    crosses_out = (cs0, cs1, cs2, cs3, cs4, cs5)
    crosses_in = (cr0, cr1, cr2, cr3, cr4, cr5)
    outs = (fg_ref, fu_ref, fd_ref)

    def fresh_rows(k, rows):
        return fresh.at[k // 2, rows, pl.ds((k % 2) * CCOL, CCOL)]

    def out_rows(k, rows):
        return outs[k // 2].at[rows, pl.ds((k % 2) * CCOL, CCOL)]

    def wide_rows(spot):
        return pl.ds(pl.multiple_of(spot * WIDE, NARROW), WIDE)

    def narrow_rows(spot):
        return pl.ds(pl.multiple_of(XY * WIDE + spot * NARROW, NARROW), NARROW)

    TALL = pl.ds(0, D - WIDE)
    TALLER = pl.ds(0, D - NARROW)
    PART = pl.ds(0, NARROW)
    MOST = pl.ds(0, SIDE - 1)

    def wait_bytes(view, sem):
        pltpu.make_async_copy(view, view, sem).wait()

    def scatter_chunk(k):
        got = gots[k]

        def to_wide(spot):
            return pltpu.make_async_remote_copy(
                src_ref=fresh_rows(k, wide_rows(spot)),
                dst_ref=got.at[local],
                send_sem=send1.at[k],
                recv_sem=recv1.at[k],
                device_id=(a, spot * ZL + wide_of),
                device_id_type=MESH,
            )

        def to_narrow(spot):
            return pltpu.make_async_remote_copy(
                src_ref=fresh_rows(k, narrow_rows(spot)),
                dst_ref=got.at[local, PART],
                send_sem=send1.at[k],
                recv_sem=recv1.at[k],
                device_id=(a, spot * ZL + narrow_of),
                device_id_type=MESH,
            )

        @pl.when(inner == 1)
        def _inner():
            pltpu.make_async_copy(fresh_rows(k, wide_rows(xy)), got.at[local], self_sem.at[k]).start()
            to_narrow(xy).start()

        @pl.when(inner == 0)
        def _outer():
            pltpu.make_async_copy(fresh_rows(k, narrow_rows(xy)), got.at[local, PART], self_sem.at[k]).start()
            to_wide(xy).start()

        def send(i, _):
            spot = ((xy // 4 + i // 4) % 4) * 4 + (xy + i) % 4
            to_wide(spot).start()
            to_narrow(spot).start()
            return _

        lax.fori_loop(1, XY, send, 0)

    def cross_copy(k, narrow):
        src, dst = crosses_out[k], crosses_in[k]
        return pltpu.make_async_remote_copy(
            src_ref=src.at[:, PART] if narrow else src,
            dst_ref=dst.at[:, PART] if narrow else dst,
            send_sem=sendx.at[k],
            recv_sem=recvx.at[k],
            device_id=(a, xy * ZL + ZL - 1 - zlo),
            device_id_type=MESH,
        )

    def cross_chunk(k):
        got, out = gots[k], crosses_out[k]

        @pl.when(inner == 1)
        def _inner():
            wait_bytes(got.at[MOST], recv1.at[k])
            pltpu.make_async_copy(fresh_rows(k, wide_rows(xy)), got.at[local], self_sem.at[k]).wait()

        @pl.when(inner == 0)
        def _outer():
            wait_bytes(got.at[MOST, PART], recv1.at[k])
            pltpu.make_async_copy(fresh_rows(k, narrow_rows(xy)), got.at[local, PART], self_sem.at[k]).wait()

        def pick(i, _):
            out[i] = got[plan_ref[0, i]]
            return _

        lax.fori_loop(0, cap, pick, 0)

        @pl.when(inner == 1)
        def _send_inner():
            cross_copy(k, False).start()

        @pl.when(inner == 0)
        def _send_outer():
            cross_copy(k, True).start()

    def regroup_chunk(k):
        got, crossed = gots[k], crosses_in[k]

        @pl.when(inner == 1)
        def _inner():
            cross_copy(k, False).wait_recv()

        @pl.when(inner == 0)
        def _outer():
            cross_copy(k, True).wait_recv()

        def pick(i, _):
            index = plan_ref[1, i]
            near = got[jnp.minimum(index, SIDE - 1)]
            far = crossed[jnp.maximum(index - SIDE, 0)]
            arr[k, i] = jnp.where(index < SIDE, near, far)
            return _

        lax.fori_loop(0, SIDE, pick, 0)

        def deliver(rows, part):
            def view(i):
                return arr.at[k, i, part] if part is not None else arr.at[k, i]

            pltpu.make_async_copy(view(local), out_rows(k, rows), self2_sem.at[k]).start()

            def send(i, _):
                spot = ((xy // 4 + i // 8) % 4) * 4 + (xy + i // 2) % 4
                end = (zlo + i) % 2
                pltpu.make_async_remote_copy(
                    src_ref=view(spot * 2 + end),
                    dst_ref=out_rows(k, rows),
                    send_sem=send2.at[k],
                    recv_sem=recv2.at[k],
                    device_id=(a, spot * ZL + side * 2 + end),
                    device_id_type=MESH,
                ).start()
                return _

            lax.fori_loop(1, SIDE, send, 0)

        @pl.when(inner == 1)
        def _deliver_inner():
            deliver(wide_rows(xy), None)

        @pl.when(inner == 0)
        def _deliver_outer():
            deliver(narrow_rows(xy), PART)

    def frame_module():
        for way in range(2):
            edge(way).wait_recv()
        has_left = jnp.where(e > 0, 1.0, 0.0)
        has_right = jnp.where(e < GROUP - 1, 1.0, 0.0)
        wide[pl.ds(0, EDGE), :] = halo[0].astype(jnp.float32) * has_left
        wide[pl.ds(EDGE + TOK, EDGE), :] = halo[1].astype(jnp.float32) * has_right
        offset = e * TOK + lax.broadcasted_iota(jnp.int32, (TOK, 1), 0)
        live = jnp.where(offset < length, 1.0, 0.0)

        def columns_step(i, _):
            columns = pl.ds(pl.multiple_of(i * 128, 128), 128)
            total = jnp.zeros((TOK, 128), jnp.float32)
            for tap in range(K):
                total = total + taps_ref[pl.ds(tap, 1), columns] * wide[pl.ds(EDGE - MARGIN + tap, TOK), columns]
            total = total + bias_ref[:, columns]
            mixed[:, columns] = (
                frames_ref[:, columns].astype(jnp.float32) + live * silu(total)
            ).astype(jnp.bfloat16)
            return _

        lax.fori_loop(0, D // 128, columns_step, 0)

        def second_norm(i, _):
            rows = pl.ds(pl.multiple_of(i * TILE, TILE), TILE)
            value = layer_norm(mixed[rows, :].astype(jnp.float32), ffn_gain_ref[...])
            agx[z, rows, :] = value.astype(jnp.bfloat16)
            return _

        lax.fori_loop(0, TOK // TILE, second_norm, 0)
        for way in range(2):
            ring(1, way).start()

        logits = lax.dot_general(
            router_ref[...], agx[z], (((1,), (1,)), ((), ())), preferred_element_type=jnp.float32
        )
        experts_iota = lax.broadcasted_iota(jnp.int32, (GROUP, TOK), 0)
        picked = [experts_iota == ids_ref[pl.ds(k, 1), :] for k in range(2)]
        named = jnp.where(picked[0] | picked[1], 1.0, 0.0).astype(jnp.bfloat16)
        before = lax.broadcasted_iota(jnp.int32, (TOK, TOK), 0) < lax.broadcasted_iota(jnp.int32, (TOK, TOK), 1)
        earlier = jnp.dot(
            named, jnp.where(before, 1.0, 0.0).astype(jnp.bfloat16), preferred_element_type=jnp.float32
        )
        lane = lax.broadcasted_iota(jnp.int32, (GROUP, GROUP), 1)
        line_of = lax.broadcasted_iota(jnp.int32, (GROUP, GROUP), 0)
        spots = (lane % ZL) * (XY * SLOTS) + (lane // ZL) * SLOTS
        place = jnp.where(resident_ref[...] == line_of, spots, 0).astype(jnp.float32)
        place = jnp.sum(place, axis=1, keepdims=True)
        limit = jnp.where(lane == line_of, capacity_ref[...], 0).astype(jnp.float32)
        limit = jnp.sum(limit, axis=1, keepdims=True)

        def of(k, values):
            return jnp.sum(jnp.where(picked[k], values, 0.0), axis=0, keepdims=True)

        scores = [1.0 / (1.0 + jnp.exp(-of(k, logits))) for k in range(2)]
        both = scores[0] + scores[1]
        for k in range(2):
            rank = of(k, earlier)
            meta_ref[pl.ds(k, 1), :] = jnp.where(rank < of(k, limit), of(k, place) + rank, -1.0)
            gate = (scores[k] / both).astype(jnp.bfloat16)
            meta_ref[pl.ds(2 + k, 1), :] = gate.astype(jnp.float32)
        meta_ref[pl.ds(4, 4), :] = jnp.zeros((4, TOK), jnp.float32)
        agm[z] = meta_ref[...]
        lax.fori_loop(1, ZN, send_meta, 0)

    def pair_blocks(p):
        first = (z - (p + 1) % HALF + ZN) % ZN
        second = (z + 1 + p) % ZN
        return first, second

    def choices(p):
        first, second = pair_blocks(p)
        ma, mb = agm[first], agm[second]
        row = lax.broadcasted_iota(jnp.int32, (ROWS, 1), 0)
        column = lax.broadcasted_iota(jnp.int32, (1, 2 * TOK), 1)
        code = (zlo * (XY * SLOTS) + (row // (2 * SLOTS)) * SLOTS + row % SLOTS).astype(jnp.float32)
        same = (row // SLOTS) % 2 == column // TOK
        both = jnp.concatenate([ma, mb], axis=1)
        hit0 = (both[0:1] == code) & same
        hit1 = (both[1:2] == code) & same
        return hit0, hit1, both

    def dispatch(p):
        first, second = pair_blocks(p)
        hit0, hit1, _ = choices(p)
        select = jnp.where(hit0 | hit1, 1.0, 0.0).astype(jnp.bfloat16)
        rows = jnp.dot(select[:, :TOK], agx[first], preferred_element_type=jnp.float32)
        rows = rows + jnp.dot(select[:, TOK:], agx[second], preferred_element_type=jnp.float32)
        pbuf[p] = rows.astype(jnp.bfloat16)
        mine = xrow.at[p, pl.ds(pl.multiple_of(xy * 2 * SLOTS, 2 * SLOTS), 2 * SLOTS)]
        pltpu.make_async_copy(
            pbuf.at[p, pl.ds(pl.multiple_of(xy * 2 * SLOTS, 2 * SLOTS), 2 * SLOTS)], mine, plane_self.at[p]
        ).start()

        def send(i, _):
            spot = (xy + i) % XY
            pltpu.make_async_remote_copy(
                src_ref=pbuf.at[p, pl.ds(pl.multiple_of(spot * 2 * SLOTS, 2 * SLOTS), 2 * SLOTS)],
                dst_ref=mine,
                send_sem=plane_send.at[p],
                recv_sem=plane_recv.at[p],
                device_id=plane(spot),
                device_id_type=MESH,
            ).start()
            return _

        lax.fori_loop(1, XY, send, 0)

    BULK = pl.ds(0, ROWS - 2 * SLOTS)
    OWN = pl.ds(pl.multiple_of(xy * 2 * SLOTS, 2 * SLOTS), 2 * SLOTS)

    def begin(k):
        refresh_chunk(k)
        scatter_chunk(k)

    scatter_chunk(0)
    begin(1)
    frame_module()
    cross_chunk(0)
    begin(2)
    for p in range(HALF):
        for way in range(2):
            ring_arrival(p + 1, way)
        if p + 2 <= HALF:
            for way in range(2):
                ring(p + 2, way).start()
        if p == 0:
            line_meta = agm.at[pl.ds(0, ZN - 1)]
            wait_bytes(line_meta, meta_recv)
        cross_chunk(p + 1)
        dispatch(p)
        if p == 0:
            begin(3)
            regroup_chunk(0)
        if p == 1:
            begin(4)
            regroup_chunk(1)
        if p == 2:
            begin(5)
            regroup_chunk(2)
        if p == 3:
            regroup_chunk(3)

    def expert_part(rows):
        gate_pre = jnp.dot(rows, fresh[0], preferred_element_type=jnp.float32) * D ** (-0.5)
        up_pre = jnp.dot(rows, fresh[1], preferred_element_type=jnp.float32) * D ** (-0.5)
        hidden = (silu(gate_pre) * up_pre).astype(jnp.bfloat16)
        return lax.dot_general(
            hidden, fresh[2], (((1,), (1,)), ((), ())), preferred_element_type=jnp.float32
        ) * FF ** (-0.5)

    def rows_copy(p):
        return pltpu.make_async_remote_copy(
            src_ref=xrow.at[p, pl.ds(0, ROWS)],
            dst_ref=xrow.at[p, pl.ds(ROWS, ROWS)],
            send_sem=x_send.at[p],
            recv_sem=x_recv.at[p],
            device_id=partner_core,
            device_id_type=MESH,
        )

    def sums_copy(p):
        return pltpu.make_async_remote_copy(
            src_ref=yoth.at[p],
            dst_ref=yin.at[p],
            send_sem=y_send.at[p],
            recv_sem=y_recv.at[p],
            device_id=partner_core,
            device_id_type=MESH,
        )

    def pass_rows(p):
        wait_bytes(xrow.at[p, BULK], plane_recv.at[p])
        pltpu.make_async_copy(pbuf.at[p, OWN], xrow.at[p, OWN], plane_self.at[p]).wait()
        rows_copy(p).start()

    def settle(p):
        sums_copy(p).wait_recv()
        yret[p] = (yown[p % 2] + yin[p].astype(jnp.float32)).astype(jnp.bfloat16)
        pltpu.make_async_copy(yret.at[p, OWN], rret.at[p, OWN], ret_self.at[p]).start()

        def send(i, _):
            spot = (xy + i) % XY
            pltpu.make_async_remote_copy(
                src_ref=yret.at[p, pl.ds(pl.multiple_of(spot * 2 * SLOTS, 2 * SLOTS), 2 * SLOTS)],
                dst_ref=rret.at[p, OWN],
                send_sem=ret_send.at[p],
                recv_sem=ret_recv.at[p],
                device_id=plane(spot),
                device_id_type=MESH,
            ).start()
            return _

        lax.fori_loop(1, XY, send, 0)

    pass_rows(0)

    def experts(p, _):
        @pl.when(p + 1 < HALF)
        def _next_rows():
            pass_rows(p + 1)

        rows_copy(p).wait_recv()
        result = expert_part(xrow[p])
        yown[p % 2] = result[:ROWS]
        yoth[p] = result[ROWS:].astype(jnp.bfloat16)
        sums_copy(p).start()

        @pl.when(p > 0)
        def _settle():
            settle(p - 1)

        @pl.when(p == 0)
        def _cross():
            cross_chunk(5)

        @pl.when(p == 2)
        def _deliver():
            regroup_chunk(4)

        return _

    lax.fori_loop(0, HALF, experts, 0)
    settle(HALF - 1)
    regroup_chunk(5)

    def combine(p, _):
        bulk = rret.at[p, BULK]
        pltpu.make_async_copy(bulk, bulk, ret_recv.at[p]).wait()
        pltpu.make_async_copy(yret.at[p, OWN], rret.at[p, OWN], ret_self.at[p]).wait()
        first, second = pair_blocks(p)
        hit0, hit1, both = choices(p)
        weights = jnp.where(hit0, both[2:3], 0.0) + jnp.where(hit1, both[3:4], 0.0)
        weights = weights.T.astype(jnp.bfloat16)
        total = jnp.dot(weights, rret[p], preferred_element_type=jnp.float32)
        part[first] = total[:TOK]
        part[second] = total[TOK:]
        return _

    lax.fori_loop(0, HALF, combine, 0)

    def rs_view(ref, step, way):
        if step == 1:
            return ref.at[way, step - 1, pl.ds(way * (TOK // 2), TOK // 2)]
        return ref.at[way, step - 1]

    def rs(step, way):
        target = line((z + 1) % ZN) if way == 0 else line((z - 1 + ZN) % ZN)
        return pltpu.make_async_remote_copy(
            src_ref=rs_view(rs_out, step, way),
            dst_ref=rs_view(rs_in, step, way),
            send_sem=rs_send.at[way, step - 1],
            recv_sem=rs_recv.at[way, step - 1],
            device_id=target,
            device_id_type=MESH,
        )

    for step in range(1, HALF + 1):
        for way in range(2):
            distance = HALF + 1 - step
            owner = (z + distance) % ZN if way == 0 else (z - distance + ZN) % ZN
            half = pl.ds(way * (TOK // 2), TOK // 2)
            other_half = pl.ds((1 - way) * (TOK // 2), TOK // 2)
            if step > 1:
                rs(step - 1, way).wait_recv()
            if step == 1:
                rs_out[way, 0, half, :] = part[owner, half, :].astype(jnp.bfloat16)
            elif step == 2:
                rs_out[way, 1, half, :] = (
                    part[owner, half, :] + rs_in[way, 0, half, :].astype(jnp.float32)
                ).astype(jnp.bfloat16)
                rs_out[way, 1, other_half, :] = part[owner, other_half, :].astype(jnp.bfloat16)
            else:
                rs_out[way, step - 1] = (
                    part[owner] + rs_in[way, step - 2].astype(jnp.float32)
                ).astype(jnp.bfloat16)
            rs(step, way).start()
    for way in range(2):
        rs(HALF, way).wait_recv()
    moe = (
        part[z]
        + rs_in[0, HALF - 1].astype(jnp.float32)
        + rs_in[1, HALF - 1].astype(jnp.float32)
    )
    out_ref[...] = (mixed[...].astype(jnp.float32) + 0.5 * moe).astype(jnp.bfloat16)

    for way in range(2):
        for step in range(1, HALF + 1):
            ring(step, way).wait_send()
            rs(step, way).wait_send()
    for way in range(2):
        edge(way).wait_send()
    for k in range(CHUNKS):

        @pl.when(inner == 1)
        def _inner():
            wait_bytes(fresh_rows(k, pl.ds(0, (XY - 1) * WIDE + XY * NARROW)), send1.at[k])
            cross_copy(k, False).wait_send()
            wait_bytes(arr.at[k, MOST], send2.at[k])
            wait_bytes(out_rows(k, TALL), recv2.at[k])
            pltpu.make_async_copy(arr.at[k, local], out_rows(k, wide_rows(xy)), self2_sem.at[k]).wait()

        @pl.when(inner == 0)
        def _outer():
            wait_bytes(fresh_rows(k, pl.ds(0, XY * WIDE + (XY - 1) * NARROW)), send1.at[k])
            cross_copy(k, True).wait_send()
            wait_bytes(arr.at[k, MOST, PART], send2.at[k])
            wait_bytes(out_rows(k, TALLER), recv2.at[k])
            pltpu.make_async_copy(arr.at[k, local, PART], out_rows(k, narrow_rows(xy)), self2_sem.at[k]).wait()

    sent_meta = agm.at[pl.ds(0, ZN - 1)]
    pltpu.make_async_copy(sent_meta, sent_meta, meta_send).wait()
    for p in range(HALF):
        bulk = pbuf.at[p, BULK]
        pltpu.make_async_copy(bulk, bulk, plane_send.at[p]).wait()
        bulk = yret.at[p, BULK]
        pltpu.make_async_copy(bulk, bulk, ret_send.at[p]).wait()
        rows_copy(p).wait_send()
        sums_copy(p).wait_send()


def plan_kernel(partner_ref, plan_ref):
    side = (lax.axis_index("expert") % ZL) // 2
    lane = lax.broadcasted_iota(jnp.int32, (GROUP, GROUP), 1)
    line_of = lax.broadcasted_iota(jnp.int32, (GROUP, GROUP), 0)

    def half_of(slot):
        return (slot % ZL) // 2

    def local_of(slot):
        return (slot // ZL) * 2 + slot % 2

    partner_row = jnp.broadcast_to(partner_ref[...], (GROUP, GROUP))
    partner_column = jnp.sum(jnp.where(lane == line_of, partner_row, 0), axis=1, keepdims=True)
    partner_column = jnp.broadcast_to(partner_column, (GROUP, GROUP))
    crossing_row = half_of(lane) != half_of(partner_row)
    crossing_column = half_of(line_of) != half_of(partner_column)

    def crossings_ahead(slot):
        ahead = (half_of(lane) == half_of(slot)) & (local_of(lane) < local_of(slot)) & crossing_row
        return jnp.sum(jnp.where(ahead, 1, 0), axis=1, keepdims=True)

    mine = half_of(line_of) == side
    sends = mine & crossing_column & (crossings_ahead(line_of) == lane)
    source = jnp.where(crossing_column, SIDE + crossings_ahead(partner_column), local_of(partner_column))
    count = jnp.sum(jnp.where(crossing_row, 1, 0), axis=1, keepdims=True) // 2
    level = jnp.broadcast_to(sum(jnp.where(count > cap, 1, 0) for cap in CAPS[:-1]), (GROUP, GROUP))
    plan_ref[pl.ds(0, 1), :] = jnp.sum(jnp.where(sends, local_of(line_of), 0), axis=0, keepdims=True)
    plan_ref[pl.ds(1, 1), :] = jnp.sum(
        jnp.where(mine & (local_of(line_of) == lane), source, 0), axis=0, keepdims=True
    )
    plan_ref[pl.ds(2, 6), :] = level[:6]


def plan(partner):
    vmem = pl.BlockSpec(memory_space=pltpu.VMEM)
    return pl.pallas_call(
        plan_kernel,
        out_shape=jax.ShapeDtypeStruct((8, GROUP), jnp.int32),
        in_specs=[vmem],
        out_specs=vmem,
    )(partner[None])


def output_kernel(*refs):
    sources, targets, buffers, in_sem, out_sem = refs[:4], refs[4:8], refs[8:12], refs[12], refs[13]
    fetch = [pltpu.make_async_copy(sources[i], buffers[i], in_sem.at[i]) for i in range(4)]
    store = [pltpu.make_async_copy(buffers[i], targets[i], out_sem.at[i]) for i in range(4)]
    for copy in fetch:
        copy.start()
    for i in range(4):
        fetch[i].wait()
        store[i].start()
    for copy in store:
        copy.wait()


def write_outputs(arrays):
    anyspace = pl.BlockSpec(memory_space=pl.ANY)
    return pl.pallas_call(
        output_kernel,
        out_shape=tuple(jax.ShapeDtypeStruct(array.shape, array.dtype) for array in arrays),
        in_specs=[anyspace] * 4,
        out_specs=(anyspace,) * 4,
        scratch_shapes=[pltpu.VMEM(array.shape, array.dtype) for array in arrays]
        + [pltpu.SemaphoreType.DMA((4,)), pltpu.SemaphoreType.DMA((4,))],
    )(*arrays)


def communicate(cap, ident, lists, length, small, weights):
    bf16, f32 = jnp.bfloat16, jnp.float32
    dma = pltpu.SemaphoreType.DMA
    vmem = pl.BlockSpec(memory_space=pltpu.VMEM)
    anyspace = pl.BlockSpec(memory_space=pl.ANY)
    moved = jax.ShapeDtypeStruct((D, FLOC), bf16)
    return pl.pallas_call(
        functools.partial(kernel, cap),
        out_shape=(jax.ShapeDtypeStruct((TOK, D), bf16), moved, moved, moved),
        in_specs=[pl.BlockSpec(memory_space=pltpu.SMEM)] * 2 + [vmem] * 9 + [anyspace] * 9,
        out_specs=(vmem, anyspace, anyspace, anyspace),
        scratch_shapes=[
            pltpu.VMEM((3, 3, D, CCOL), bf16),
            pltpu.VMEM((3, D, FLOC), bf16),
            pltpu.VMEM((TOK + 2 * EDGE, D), f32),
            pltpu.VMEM((TOK, D), bf16),
            pltpu.VMEM((2, EDGE, D), bf16),
            pltpu.VMEM((TOK, D), bf16),
            pltpu.VMEM((8, TOK), f32),
        ]
        + [pltpu.VMEM((SIDE, WIDE, CCOL), bf16)] * CHUNKS
        + [pltpu.VMEM((cap, WIDE, CCOL), bf16)] * (2 * CHUNKS)
        + [
            pltpu.VMEM((CHUNKS, SIDE, WIDE, CCOL), bf16),
            pltpu.VMEM((ZN, TOK, D), bf16),
            pltpu.VMEM((ZN, 8, TOK), f32),
            pltpu.VMEM((HALF, ROWS, D), bf16),
            pltpu.VMEM((HALF, 2 * ROWS, D), bf16),
            pltpu.VMEM((2, ROWS, D), f32),
            pltpu.VMEM((HALF, ROWS, D), bf16),
            pltpu.VMEM((HALF, ROWS, D), bf16),
            pltpu.VMEM((HALF, ROWS, D), bf16),
            pltpu.VMEM((HALF, ROWS, D), bf16),
            pltpu.VMEM((ZN, TOK, D), f32),
            pltpu.VMEM((2, HALF, TOK, D), bf16),
            pltpu.VMEM((2, HALF, TOK, D), bf16),
            dma((2,)),
            dma((2,)),
            dma((3, 3)),
            dma((CHUNKS,)),
            dma((CHUNKS,)),
            dma((CHUNKS,)),
            dma((CHUNKS,)),
            dma((CHUNKS,)),
            dma((CHUNKS,)),
            dma((CHUNKS,)),
            dma((CHUNKS,)),
            dma((2, HALF)),
            dma((2, HALF)),
            dma,
            dma,
            dma((HALF,)),
            dma((HALF,)),
            dma((HALF,)),
            dma((HALF,)),
            dma((HALF,)),
            dma((HALF,)),
            dma((HALF,)),
            dma((HALF,)),
            dma((HALF,)),
            dma((HALF,)),
            dma((2, HALF)),
            dma((2, HALF)),
        ],
        compiler_params=pltpu.CompilerParams(
            collective_id=ident, has_side_effects=True, vmem_limit_bytes=64 * 1024 * 1024 - 65536
        ),
    )(lists, length, *small, *weights)


def shards(
    frames,
    lengths,
    expert_ids,
    capacity,
    resident,
    partner,
    conv_gain,
    conv_kernel,
    conv_bias,
    ffn_gain,
    router,
    gate_weight,
    up_weight,
    down_weight,
    gate_mean_grad,
    gate_mean_square,
    up_mean_grad,
    up_mean_square,
    down_mean_grad,
    down_mean_square,
):
    lists = plan(partner)
    operands = (
        lists,
        lengths,
        (
            frames,
            expert_ids.T,
            resident[None],
            capacity[None],
            conv_gain[None],
            conv_kernel,
            conv_bias[None],
            ffn_gain[None],
            router.T,
        ),
        (
            gate_weight[0], gate_mean_grad[0], gate_mean_square[0],
            up_weight[0], up_mean_grad[0], up_mean_square[0],
            down_weight[0], down_mean_grad[0], down_mean_square[0],
        ),
    )
    block_out, fresh_gate, fresh_up, fresh_down = lax.switch(
        lists[2, 0],
        [
            lambda operands, cap=cap, ident=ident: communicate(cap, ident, *operands)
            for ident, cap in enumerate(CAPS)
        ],
        operands,
    )
    block_out, fresh_gate, fresh_up, fresh_down = write_outputs(
        (block_out, fresh_gate, fresh_up, fresh_down)
    )
    return (block_out, fresh_gate[None], fresh_up[None], fresh_down[None])


def solution(mesh):
    placed = (
        P(("dp", "expert"), None),
        P("dp"),
        P(("dp", "expert"), None),
        P(),
        P(),
        P(),
        P(),
        P(),
        P(),
        P(),
        P(),
        P("expert", None, "dp"),
        P("expert", None, "dp"),
        P("expert", None, "dp"),
        P("expert", None, "dp"),
        P("expert", None, "dp"),
        P("expert", None, "dp"),
        P("expert", None, "dp"),
        P("expert", None, "dp"),
        P("expert", None, "dp"),
    )
    return jax.shard_map(
        shards,
        mesh=mesh,
        in_specs=placed,
        out_specs=(
            P(("dp", "expert"), None),
            P("expert", None, "dp"),
            P("expert", None, "dp"),
            P("expert", None, "dp"),
        ),
        check_vma=False,
    )
```

```python
import functools

import jax
import jax.numpy as jnp
from jax import lax
from jax.experimental import pallas as pl
from jax.experimental.pallas import tpu as pltpu
from jax.sharding import PartitionSpec as P

D = 1024
FF = 2048
K = 31


LEARNING_RATE = 0.1
ADAM_EPSILON = 1e-08
NORM_EPSILON = 1e-05

MESH = pl.DeviceIdType.MESH
XY = 16
ZL = 4
ZN = 8
HALF = ZN // 2
GROUP = XY * ZL
SLOTS = 8
TOK = 128
FLOC = 512
ROWS = XY * 2 * SLOTS
SIDE = GROUP // 2
WIDE = 48
NARROW = 16
CHUNKS = 6
CCOL = FLOC // 2
MARGIN = (K - 1) // 2
EDGE = 16
TILE = 32
CAPS = (18, 22, SIDE)


def layer_norm(values, gain_row):
    centred = values - jnp.mean(values, axis=-1, keepdims=True)
    variance = jnp.mean(centred * centred, axis=-1, keepdims=True)
    return centred * lax.rsqrt(variance + NORM_EPSILON) * gain_row


def refresh(weight, first_moment, second_moment):
    step_size = (
        LEARNING_RATE
        * first_moment.astype(jnp.float32)
        / (jnp.sqrt(second_moment.astype(jnp.float32)) + ADAM_EPSILON)
    )
    return (weight.astype(jnp.float32) - step_size).astype(jnp.bfloat16)


def silu(value):
    return value / (1.0 + jnp.exp(-value))


def kernel(
    cap,
    plan_ref,
    length_ref,
    frames_ref,
    ids_ref,
    resident_ref,
    capacity_ref,
    conv_gain_ref,
    taps_ref,
    bias_ref,
    ffn_gain_ref,
    router_ref,
    gw, gm, gs, uw, um, us, dw, dm, ds,
    out_ref,
    fg_ref,
    fu_ref,
    fd_ref,
    win,
    fresh,
    wide,
    normed,
    halo,
    mixed,
    meta_ref,
    got0, got1, got2, got3, got4, got5,
    cs0, cs1, cs2, cs3, cs4, cs5,
    cr0, cr1, cr2, cr3, cr4, cr5,
    arr,
    agx,
    agm,
    pbuf,
    xrow,
    yown,
    yoth,
    yin,
    yret,
    rret,
    part,
    rs_out,
    rs_in,
    halo_send,
    halo_recv,
    load_sem,
    self_sem,
    self2_sem,
    send1,
    recv1,
    sendx,
    recvx,
    send2,
    recv2,
    ring_send,
    ring_recv,
    meta_send,
    meta_recv,
    plane_send,
    plane_recv,
    plane_self,
    x_send,
    x_recv,
    y_send,
    y_recv,
    ret_send,
    ret_recv,
    ret_self,
    rs_send,
    rs_recv,
):
    a = lax.axis_index("dp")
    e = lax.axis_index("expert")
    core = a % 2
    zlo = e % ZL
    xy = e // ZL
    z = (a // 2) * ZL + zlo
    side = zlo // 2
    inner = ((zlo + 1) // 2) % 2
    local = xy * 2 + zlo % 2
    wide_of = 1 + side
    narrow_of = 3 * side

    def line(position):
        return ((position // ZL) * 2 + core, xy * ZL + position % ZL)

    def plane(spot):
        return (a, spot * ZL + zlo)

    partner_core = ((a // 2) * 2 + 1 - core, e)

    barrier = pltpu.get_barrier_semaphore()

    def greet_group(i, _):
        pl.semaphore_signal(barrier, inc=1, device_id=(a, (e + i) % GROUP), device_id_type=MESH)
        return _

    lax.fori_loop(1, GROUP, greet_group, 0)

    def greet_line(i, _):
        far = (1 - a // 2) * ZL + i
        pl.semaphore_signal(barrier, inc=1, device_id=line(far), device_id_type=MESH)
        return _

    lax.fori_loop(0, ZL, greet_line, 0)
    pl.semaphore_signal(barrier, inc=1, device_id=partner_core, device_id_type=MESH)

    sources = ((gw, gm, gs), (uw, um, us), (dw, dm, ds))

    def load(c, i):
        columns = pl.ds((c % 2) * CCOL, CCOL)
        return pltpu.make_async_copy(
            sources[c // 2][i].at[:, columns], win.at[c % 3, i], load_sem.at[c % 3, i]
        )

    for c in range(3):
        for i in range(3):
            load(c, i).start()

    def refresh_chunk(k):
        for i in range(3):
            load(k, i).wait()
        slot = k % 3

        def tile(i, _):
            rows = pl.ds(pl.multiple_of(i * 64, 64), 64)
            fresh[k // 2, rows, pl.ds((k % 2) * CCOL, CCOL)] = refresh(
                win[slot, 0, rows, :], win[slot, 1, rows, :], win[slot, 2, rows, :]
            )
            return _

        lax.fori_loop(0, D // 64, tile, 0)
        if k + 3 < CHUNKS:
            for i in range(3):
                load(k + 3, i).start()

    refresh_chunk(0)

    length = length_ref[0]

    def first_norm(i, _):
        rows = pl.ds(pl.multiple_of(i * TILE, TILE), TILE)
        offset = e * TOK + i * TILE + lax.broadcasted_iota(jnp.int32, (TILE, 1), 0)
        live = jnp.where(offset < length, 1.0, 0.0)
        value = layer_norm(frames_ref[rows, :].astype(jnp.float32), conv_gain_ref[...]) * live
        value = value.astype(jnp.bfloat16)
        normed[rows, :] = value
        wide[pl.ds(pl.multiple_of(EDGE + i * TILE, EDGE), TILE), :] = value.astype(jnp.float32)
        return _

    lax.fori_loop(0, TOK // TILE, first_norm, 0)
    pl.semaphore_wait(barrier, GROUP + ZL)

    def edge(way):
        start = TOK - EDGE if way == 0 else 0
        neighbour = (e + 1) % GROUP if way == 0 else (e - 1 + GROUP) % GROUP
        return pltpu.make_async_remote_copy(
            src_ref=normed.at[pl.ds(start, EDGE)],
            dst_ref=halo.at[way],
            send_sem=halo_send.at[way],
            recv_sem=halo_recv.at[way],
            device_id=(a, neighbour),
            device_id_type=MESH,
        )

    for way in range(2):
        edge(way).start()

    def ring(step, way):
        if way == 0:
            block = (z - step + 1 + ZN) % ZN
            target = line((z + 1) % ZN)
        else:
            block = (z + step - 1) % ZN
            target = line((z - 1 + ZN) % ZN)
        if step == HALF:
            view = agx.at[block, pl.ds(way * (TOK // 2), TOK // 2)]
        else:
            view = agx.at[block]
        return pltpu.make_async_remote_copy(
            src_ref=view,
            dst_ref=view,
            send_sem=ring_send.at[way, step - 1],
            recv_sem=ring_recv.at[way, step - 1],
            device_id=target,
            device_id_type=MESH,
        )

    def ring_arrival(step, way):
        if way == 0:
            block = (z - step + ZN) % ZN
        else:
            block = (z + step) % ZN
        if step == HALF:
            view = agx.at[block, pl.ds(way * (TOK // 2), TOK // 2)]
        else:
            view = agx.at[block]
        pltpu.make_async_copy(view, view, ring_recv.at[way, step - 1]).wait()

    def meta_copy(i):
        return pltpu.make_async_remote_copy(
            src_ref=meta_ref,
            dst_ref=agm.at[z],
            send_sem=meta_send,
            recv_sem=meta_recv,
            device_id=line((z + i) % ZN),
            device_id_type=MESH,
        )

    def send_meta(i, _):
        meta_copy(i).start()
        return _

    gots = (got0, got1, got2, got3, got4, got5)
    crosses_out = (cs0, cs1, cs2, cs3, cs4, cs5)
    crosses_in = (cr0, cr1, cr2, cr3, cr4, cr5)
    outs = (fg_ref, fu_ref, fd_ref)

    def fresh_rows(k, rows):
        return fresh.at[k // 2, rows, pl.ds((k % 2) * CCOL, CCOL)]

    def out_rows(k, rows):
        return outs[k // 2].at[rows, pl.ds((k % 2) * CCOL, CCOL)]

    def wide_rows(spot):
        return pl.ds(pl.multiple_of(spot * WIDE, NARROW), WIDE)

    def narrow_rows(spot):
        return pl.ds(pl.multiple_of(XY * WIDE + spot * NARROW, NARROW), NARROW)

    TALL = pl.ds(0, D - WIDE)
    TALLER = pl.ds(0, D - NARROW)
    PART = pl.ds(0, NARROW)
    MOST = pl.ds(0, SIDE - 1)

    def wait_bytes(view, sem):
        pltpu.make_async_copy(view, view, sem).wait()

    def scatter_chunk(k):
        got = gots[k]

        def to_wide(spot):
            return pltpu.make_async_remote_copy(
                src_ref=fresh_rows(k, wide_rows(spot)),
                dst_ref=got.at[local],
                send_sem=send1.at[k],
                recv_sem=recv1.at[k],
                device_id=(a, spot * ZL + wide_of),
                device_id_type=MESH,
            )

        def to_narrow(spot):
            return pltpu.make_async_remote_copy(
                src_ref=fresh_rows(k, narrow_rows(spot)),
                dst_ref=got.at[local, PART],
                send_sem=send1.at[k],
                recv_sem=recv1.at[k],
                device_id=(a, spot * ZL + narrow_of),
                device_id_type=MESH,
            )

        @pl.when(inner == 1)
        def _inner():
            pltpu.make_async_copy(fresh_rows(k, wide_rows(xy)), got.at[local], self_sem.at[k]).start()
            to_narrow(xy).start()

        @pl.when(inner == 0)
        def _outer():
            pltpu.make_async_copy(fresh_rows(k, narrow_rows(xy)), got.at[local, PART], self_sem.at[k]).start()
            to_wide(xy).start()

        def send(i, _):
            spot = ((xy // 4 + i // 4) % 4) * 4 + (xy + i) % 4
            to_wide(spot).start()
            to_narrow(spot).start()
            return _

        lax.fori_loop(1, XY, send, 0)

    def cross_copy(k, narrow):
        src, dst = crosses_out[k], crosses_in[k]
        return pltpu.make_async_remote_copy(
            src_ref=src.at[:, PART] if narrow else src,
            dst_ref=dst.at[:, PART] if narrow else dst,
            send_sem=sendx.at[k],
            recv_sem=recvx.at[k],
            device_id=(a, xy * ZL + ZL - 1 - zlo),
            device_id_type=MESH,
        )

    def cross_chunk(k):
        got, out = gots[k], crosses_out[k]

        @pl.when(inner == 1)
        def _inner():
            wait_bytes(got.at[MOST], recv1.at[k])
            pltpu.make_async_copy(fresh_rows(k, wide_rows(xy)), got.at[local], self_sem.at[k]).wait()

        @pl.when(inner == 0)
        def _outer():
            wait_bytes(got.at[MOST, PART], recv1.at[k])
            pltpu.make_async_copy(fresh_rows(k, narrow_rows(xy)), got.at[local, PART], self_sem.at[k]).wait()

        def pick(i, _):
            out[i] = got[plan_ref[0, i]]
            return _

        lax.fori_loop(0, cap, pick, 0)

        @pl.when(inner == 1)
        def _send_inner():
            cross_copy(k, False).start()

        @pl.when(inner == 0)
        def _send_outer():
            cross_copy(k, True).start()

    def regroup_chunk(k):
        got, crossed = gots[k], crosses_in[k]

        @pl.when(inner == 1)
        def _inner():
            cross_copy(k, False).wait_recv()

        @pl.when(inner == 0)
        def _outer():
            cross_copy(k, True).wait_recv()

        def pick(i, _):
            index = plan_ref[1, i]
            near = got[jnp.minimum(index, SIDE - 1)]
            far = crossed[jnp.maximum(index - SIDE, 0)]
            arr[k, i] = jnp.where(index < SIDE, near, far)
            return _

        lax.fori_loop(0, SIDE, pick, 0)

        def deliver(rows, part):
            def view(i):
                return arr.at[k, i, part] if part is not None else arr.at[k, i]

            pltpu.make_async_copy(view(local), out_rows(k, rows), self2_sem.at[k]).start()

            def send(i, _):
                spot = ((xy // 4 + i // 8) % 4) * 4 + (xy + i // 2) % 4
                end = (zlo + i) % 2
                pltpu.make_async_remote_copy(
                    src_ref=view(spot * 2 + end),
                    dst_ref=out_rows(k, rows),
                    send_sem=send2.at[k],
                    recv_sem=recv2.at[k],
                    device_id=(a, spot * ZL + side * 2 + end),
                    device_id_type=MESH,
                ).start()
                return _

            lax.fori_loop(1, SIDE, send, 0)

        @pl.when(inner == 1)
        def _deliver_inner():
            deliver(wide_rows(xy), None)

        @pl.when(inner == 0)
        def _deliver_outer():
            deliver(narrow_rows(xy), PART)

    def frame_module():
        for way in range(2):
            edge(way).wait_recv()
        has_left = jnp.where(e > 0, 1.0, 0.0)
        has_right = jnp.where(e < GROUP - 1, 1.0, 0.0)
        wide[pl.ds(0, EDGE), :] = halo[0].astype(jnp.float32) * has_left
        wide[pl.ds(EDGE + TOK, EDGE), :] = halo[1].astype(jnp.float32) * has_right
        offset = e * TOK + lax.broadcasted_iota(jnp.int32, (TOK, 1), 0)
        live = jnp.where(offset < length, 1.0, 0.0)

        def columns_step(i, _):
            columns = pl.ds(pl.multiple_of(i * 128, 128), 128)
            total = jnp.zeros((TOK, 128), jnp.float32)
            for tap in range(K):
                total = total + taps_ref[pl.ds(tap, 1), columns] * wide[pl.ds(EDGE - MARGIN + tap, TOK), columns]
            total = total + bias_ref[:, columns]
            mixed[:, columns] = (
                frames_ref[:, columns].astype(jnp.float32) + live * silu(total)
            ).astype(jnp.bfloat16)
            return _

        lax.fori_loop(0, D // 128, columns_step, 0)

        def second_norm(i, _):
            rows = pl.ds(pl.multiple_of(i * TILE, TILE), TILE)
            value = layer_norm(mixed[rows, :].astype(jnp.float32), ffn_gain_ref[...])
            agx[z, rows, :] = value.astype(jnp.bfloat16)
            return _

        lax.fori_loop(0, TOK // TILE, second_norm, 0)
        for way in range(2):
            ring(1, way).start()

        logits = lax.dot_general(
            router_ref[...], agx[z], (((1,), (1,)), ((), ())), preferred_element_type=jnp.float32
        )
        experts_iota = lax.broadcasted_iota(jnp.int32, (GROUP, TOK), 0)
        picked = [experts_iota == ids_ref[pl.ds(k, 1), :] for k in range(2)]
        named = jnp.where(picked[0] | picked[1], 1.0, 0.0).astype(jnp.bfloat16)
        before = lax.broadcasted_iota(jnp.int32, (TOK, TOK), 0) < lax.broadcasted_iota(jnp.int32, (TOK, TOK), 1)
        earlier = jnp.dot(
            named, jnp.where(before, 1.0, 0.0).astype(jnp.bfloat16), preferred_element_type=jnp.float32
        )
        lane = lax.broadcasted_iota(jnp.int32, (GROUP, GROUP), 1)
        line_of = lax.broadcasted_iota(jnp.int32, (GROUP, GROUP), 0)
        spots = (lane % ZL) * (XY * SLOTS) + (lane // ZL) * SLOTS
        place = jnp.where(resident_ref[...] == line_of, spots, 0).astype(jnp.float32)
        place = jnp.sum(place, axis=1, keepdims=True)
        limit = jnp.where(lane == line_of, capacity_ref[...], 0).astype(jnp.float32)
        limit = jnp.sum(limit, axis=1, keepdims=True)

        def of(k, values):
            return jnp.sum(jnp.where(picked[k], values, 0.0), axis=0, keepdims=True)

        scores = [1.0 / (1.0 + jnp.exp(-of(k, logits))) for k in range(2)]
        both = scores[0] + scores[1]
        for k in range(2):
            rank = of(k, earlier)
            meta_ref[pl.ds(k, 1), :] = jnp.where(rank < of(k, limit), of(k, place) + rank, -1.0)
            gate = (scores[k] / both).astype(jnp.bfloat16)
            meta_ref[pl.ds(2 + k, 1), :] = gate.astype(jnp.float32)
        meta_ref[pl.ds(4, 4), :] = jnp.zeros((4, TOK), jnp.float32)
        agm[z] = meta_ref[...]
        lax.fori_loop(1, ZN, send_meta, 0)

    def pair_blocks(p):
        first = (z - (p + 1) % HALF + ZN) % ZN
        second = (z + 1 + p) % ZN
        return first, second

    def choices(p):
        first, second = pair_blocks(p)
        ma, mb = agm[first], agm[second]
        row = lax.broadcasted_iota(jnp.int32, (ROWS, 1), 0)
        column = lax.broadcasted_iota(jnp.int32, (1, 2 * TOK), 1)
        code = (zlo * (XY * SLOTS) + (row // (2 * SLOTS)) * SLOTS + row % SLOTS).astype(jnp.float32)
        same = (row // SLOTS) % 2 == column // TOK
        both = jnp.concatenate([ma, mb], axis=1)
        hit0 = (both[0:1] == code) & same
        hit1 = (both[1:2] == code) & same
        return hit0, hit1, both

    def dispatch(p):
        first, second = pair_blocks(p)
        hit0, hit1, _ = choices(p)
        select = jnp.where(hit0 | hit1, 1.0, 0.0).astype(jnp.bfloat16)
        rows = jnp.dot(select[:, :TOK], agx[first], preferred_element_type=jnp.float32)
        rows = rows + jnp.dot(select[:, TOK:], agx[second], preferred_element_type=jnp.float32)
        pbuf[p] = rows.astype(jnp.bfloat16)
        mine = xrow.at[p, pl.ds(pl.multiple_of(xy * 2 * SLOTS, 2 * SLOTS), 2 * SLOTS)]
        pltpu.make_async_copy(
            pbuf.at[p, pl.ds(pl.multiple_of(xy * 2 * SLOTS, 2 * SLOTS), 2 * SLOTS)], mine, plane_self.at[p]
        ).start()

        def send(i, _):
            spot = (xy + i) % XY
            pltpu.make_async_remote_copy(
                src_ref=pbuf.at[p, pl.ds(pl.multiple_of(spot * 2 * SLOTS, 2 * SLOTS), 2 * SLOTS)],
                dst_ref=mine,
                send_sem=plane_send.at[p],
                recv_sem=plane_recv.at[p],
                device_id=plane(spot),
                device_id_type=MESH,
            ).start()
            return _

        lax.fori_loop(1, XY, send, 0)

    BULK = pl.ds(0, ROWS - 2 * SLOTS)
    OWN = pl.ds(pl.multiple_of(xy * 2 * SLOTS, 2 * SLOTS), 2 * SLOTS)

    def begin(k):
        refresh_chunk(k)
        scatter_chunk(k)

    scatter_chunk(0)
    begin(1)
    frame_module()
    cross_chunk(0)
    begin(2)
    for p in range(HALF):
        for way in range(2):
            ring_arrival(p + 1, way)
        if p + 2 <= HALF:
            for way in range(2):
                ring(p + 2, way).start()
        if p == 0:
            line_meta = agm.at[pl.ds(0, ZN - 1)]
            wait_bytes(line_meta, meta_recv)
        if p == 0:
            cross_chunk(1)
        if p == 1:
            cross_chunk(2)
        if p == 2:
            cross_chunk(3)
        if p == 3:
            cross_chunk(4)
        dispatch(p)
        if p == 0:
            begin(3)
            regroup_chunk(0)
        if p == 1:
            begin(4)
            regroup_chunk(1)
        if p == 2:
            begin(5)
            regroup_chunk(2)
        if p == 3:
            regroup_chunk(3)

    def expert_part(rows):
        gate_pre = jnp.dot(rows, fresh[0], preferred_element_type=jnp.float32) * D ** (-0.5)
        up_pre = jnp.dot(rows, fresh[1], preferred_element_type=jnp.float32) * D ** (-0.5)
        hidden = (silu(gate_pre) * up_pre).astype(jnp.bfloat16)
        return lax.dot_general(
            hidden, fresh[2], (((1,), (1,)), ((), ())), preferred_element_type=jnp.float32
        ) * FF ** (-0.5)

    def rows_copy(p):
        return pltpu.make_async_remote_copy(
            src_ref=xrow.at[p, pl.ds(0, ROWS)],
            dst_ref=xrow.at[p, pl.ds(ROWS, ROWS)],
            send_sem=x_send.at[p],
            recv_sem=x_recv.at[p],
            device_id=partner_core,
            device_id_type=MESH,
        )

    def sums_copy(p):
        return pltpu.make_async_remote_copy(
            src_ref=yoth.at[p],
            dst_ref=yin.at[p],
            send_sem=y_send.at[p],
            recv_sem=y_recv.at[p],
            device_id=partner_core,
            device_id_type=MESH,
        )

    def pass_rows(p):
        wait_bytes(xrow.at[p, BULK], plane_recv.at[p])
        pltpu.make_async_copy(pbuf.at[p, OWN], xrow.at[p, OWN], plane_self.at[p]).wait()
        rows_copy(p).start()

    def settle(p):
        sums_copy(p).wait_recv()
        yret[p] = (yown[p % 2] + yin[p].astype(jnp.float32)).astype(jnp.bfloat16)
        pltpu.make_async_copy(yret.at[p, OWN], rret.at[p, OWN], ret_self.at[p]).start()

        def send(i, _):
            spot = (xy + i) % XY
            pltpu.make_async_remote_copy(
                src_ref=yret.at[p, pl.ds(pl.multiple_of(spot * 2 * SLOTS, 2 * SLOTS), 2 * SLOTS)],
                dst_ref=rret.at[p, OWN],
                send_sem=ret_send.at[p],
                recv_sem=ret_recv.at[p],
                device_id=plane(spot),
                device_id_type=MESH,
            ).start()
            return _

        lax.fori_loop(1, XY, send, 0)

    pass_rows(0)

    def experts(p, _):
        @pl.when(p + 1 < HALF)
        def _next_rows():
            pass_rows(p + 1)

        rows_copy(p).wait_recv()
        result = expert_part(xrow[p])
        yown[p % 2] = result[:ROWS]
        yoth[p] = result[ROWS:].astype(jnp.bfloat16)
        sums_copy(p).start()

        @pl.when(p > 0)
        def _settle():
            settle(p - 1)

        @pl.when(p == 0)
        def _slot0():
            cross_chunk(5)

        @pl.when(p == 2)
        def _slot2():
            regroup_chunk(4)

        return _

    lax.fori_loop(0, HALF, experts, 0)
    settle(HALF - 1)
    regroup_chunk(5)

    def combine(p):
        bulk = rret.at[p, BULK]
        pltpu.make_async_copy(bulk, bulk, ret_recv.at[p]).wait()
        pltpu.make_async_copy(yret.at[p, OWN], rret.at[p, OWN], ret_self.at[p]).wait()
        first, second = pair_blocks(p)
        hit0, hit1, both = choices(p)
        weights = jnp.where(hit0, both[2:3], 0.0) + jnp.where(hit1, both[3:4], 0.0)
        weights = weights.T.astype(jnp.bfloat16)
        total = jnp.dot(weights, rret[p], preferred_element_type=jnp.float32)
        part[first] = total[:TOK]
        part[second] = total[TOK:]

    def rs_view(ref, step, way):
        if step == 1:
            return ref.at[way, step - 1, pl.ds(way * (TOK // 2), TOK // 2)]
        return ref.at[way, step - 1]

    def rs(step, way):
        target = line((z + 1) % ZN) if way == 0 else line((z - 1 + ZN) % ZN)
        return pltpu.make_async_remote_copy(
            src_ref=rs_view(rs_out, step, way),
            dst_ref=rs_view(rs_in, step, way),
            send_sem=rs_send.at[way, step - 1],
            recv_sem=rs_recv.at[way, step - 1],
            device_id=target,
            device_id_type=MESH,
        )

    for step in range(1, HALF + 1):
        combine(HALF - step)
        for way in range(2):
            distance = HALF + 1 - step
            owner = (z + distance) % ZN if way == 0 else (z - distance + ZN) % ZN
            half = pl.ds(way * (TOK // 2), TOK // 2)
            other_half = pl.ds((1 - way) * (TOK // 2), TOK // 2)
            if step > 1:
                rs(step - 1, way).wait_recv()
            if step == 1:
                rs_out[way, 0, half, :] = part[owner, half, :].astype(jnp.bfloat16)
            elif step == 2:
                rs_out[way, 1, half, :] = (
                    part[owner, half, :] + rs_in[way, 0, half, :].astype(jnp.float32)
                ).astype(jnp.bfloat16)
                rs_out[way, 1, other_half, :] = part[owner, other_half, :].astype(jnp.bfloat16)
            else:
                rs_out[way, step - 1] = (
                    part[owner] + rs_in[way, step - 2].astype(jnp.float32)
                ).astype(jnp.bfloat16)
            rs(step, way).start()
    for way in range(2):
        rs(HALF, way).wait_recv()
    moe = (
        part[z]
        + rs_in[0, HALF - 1].astype(jnp.float32)
        + rs_in[1, HALF - 1].astype(jnp.float32)
    )
    out_ref[...] = (mixed[...].astype(jnp.float32) + 0.5 * moe).astype(jnp.bfloat16)

    for way in range(2):
        for step in range(1, HALF + 1):
            ring(step, way).wait_send()
            rs(step, way).wait_send()
    for way in range(2):
        edge(way).wait_send()
    for k in range(CHUNKS):

        @pl.when(inner == 1)
        def _inner():
            wait_bytes(fresh_rows(k, pl.ds(0, (XY - 1) * WIDE + XY * NARROW)), send1.at[k])
            cross_copy(k, False).wait_send()
            wait_bytes(arr.at[k, MOST], send2.at[k])
            wait_bytes(out_rows(k, TALL), recv2.at[k])
            pltpu.make_async_copy(arr.at[k, local], out_rows(k, wide_rows(xy)), self2_sem.at[k]).wait()

        @pl.when(inner == 0)
        def _outer():
            wait_bytes(fresh_rows(k, pl.ds(0, XY * WIDE + (XY - 1) * NARROW)), send1.at[k])
            cross_copy(k, True).wait_send()
            wait_bytes(arr.at[k, MOST, PART], send2.at[k])
            wait_bytes(out_rows(k, TALLER), recv2.at[k])
            pltpu.make_async_copy(arr.at[k, local, PART], out_rows(k, narrow_rows(xy)), self2_sem.at[k]).wait()

    sent_meta = agm.at[pl.ds(0, ZN - 1)]
    pltpu.make_async_copy(sent_meta, sent_meta, meta_send).wait()
    for p in range(HALF):
        bulk = pbuf.at[p, BULK]
        pltpu.make_async_copy(bulk, bulk, plane_send.at[p]).wait()
        bulk = yret.at[p, BULK]
        pltpu.make_async_copy(bulk, bulk, ret_send.at[p]).wait()
        rows_copy(p).wait_send()
        sums_copy(p).wait_send()


def plan_kernel(partner_ref, plan_ref):
    side = (lax.axis_index("expert") % ZL) // 2
    lane = lax.broadcasted_iota(jnp.int32, (GROUP, GROUP), 1)
    line_of = lax.broadcasted_iota(jnp.int32, (GROUP, GROUP), 0)

    def half_of(slot):
        return (slot % ZL) // 2

    def local_of(slot):
        return (slot // ZL) * 2 + slot % 2

    partner_row = jnp.broadcast_to(partner_ref[...], (GROUP, GROUP))
    partner_column = jnp.sum(jnp.where(lane == line_of, partner_row, 0), axis=1, keepdims=True)
    partner_column = jnp.broadcast_to(partner_column, (GROUP, GROUP))
    crossing_row = half_of(lane) != half_of(partner_row)
    crossing_column = half_of(line_of) != half_of(partner_column)

    def crossings_ahead(slot):
        ahead = (half_of(lane) == half_of(slot)) & (local_of(lane) < local_of(slot)) & crossing_row
        return jnp.sum(jnp.where(ahead, 1, 0), axis=1, keepdims=True)

    mine = half_of(line_of) == side
    sends = mine & crossing_column & (crossings_ahead(line_of) == lane)
    source = jnp.where(crossing_column, SIDE + crossings_ahead(partner_column), local_of(partner_column))
    count = jnp.sum(jnp.where(crossing_row, 1, 0), axis=1, keepdims=True) // 2
    level = jnp.broadcast_to(sum(jnp.where(count > cap, 1, 0) for cap in CAPS[:-1]), (GROUP, GROUP))
    plan_ref[pl.ds(0, 1), :] = jnp.sum(jnp.where(sends, local_of(line_of), 0), axis=0, keepdims=True)
    plan_ref[pl.ds(1, 1), :] = jnp.sum(
        jnp.where(mine & (local_of(line_of) == lane), source, 0), axis=0, keepdims=True
    )
    plan_ref[pl.ds(2, 6), :] = level[:6]


def plan(partner):
    vmem = pl.BlockSpec(memory_space=pltpu.VMEM)
    return pl.pallas_call(
        plan_kernel,
        out_shape=jax.ShapeDtypeStruct((8, GROUP), jnp.int32),
        in_specs=[vmem],
        out_specs=vmem,
    )(partner[None])


def output_kernel(*refs):
    sources, targets, buffers, in_sem, out_sem = refs[:4], refs[4:8], refs[8:12], refs[12], refs[13]
    fetch = [pltpu.make_async_copy(sources[i], buffers[i], in_sem.at[i]) for i in range(4)]
    store = [pltpu.make_async_copy(buffers[i], targets[i], out_sem.at[i]) for i in range(4)]
    for copy in fetch:
        copy.start()
    for i in range(4):
        fetch[i].wait()
        store[i].start()
    for copy in store:
        copy.wait()


def write_outputs(arrays):
    anyspace = pl.BlockSpec(memory_space=pl.ANY)
    return pl.pallas_call(
        output_kernel,
        out_shape=tuple(jax.ShapeDtypeStruct(array.shape, array.dtype) for array in arrays),
        in_specs=[anyspace] * 4,
        out_specs=(anyspace,) * 4,
        scratch_shapes=[pltpu.VMEM(array.shape, array.dtype) for array in arrays]
        + [pltpu.SemaphoreType.DMA((4,)), pltpu.SemaphoreType.DMA((4,))],
    )(*arrays)


def communicate(cap, ident, lists, length, small, weights):
    bf16, f32 = jnp.bfloat16, jnp.float32
    dma = pltpu.SemaphoreType.DMA
    vmem = pl.BlockSpec(memory_space=pltpu.VMEM)
    anyspace = pl.BlockSpec(memory_space=pl.ANY)
    moved = jax.ShapeDtypeStruct((D, FLOC), bf16)
    return pl.pallas_call(
        functools.partial(kernel, cap),
        out_shape=(jax.ShapeDtypeStruct((TOK, D), bf16), moved, moved, moved),
        in_specs=[pl.BlockSpec(memory_space=pltpu.SMEM)] * 2 + [vmem] * 9 + [anyspace] * 9,
        out_specs=(vmem, anyspace, anyspace, anyspace),
        scratch_shapes=[
            pltpu.VMEM((3, 3, D, CCOL), bf16),
            pltpu.VMEM((3, D, FLOC), bf16),
            pltpu.VMEM((TOK + 2 * EDGE, D), f32),
            pltpu.VMEM((TOK, D), bf16),
            pltpu.VMEM((2, EDGE, D), bf16),
            pltpu.VMEM((TOK, D), bf16),
            pltpu.VMEM((8, TOK), f32),
        ]
        + [pltpu.VMEM((SIDE, WIDE, CCOL), bf16)] * CHUNKS
        + [pltpu.VMEM((cap, WIDE, CCOL), bf16)] * (2 * CHUNKS)
        + [
            pltpu.VMEM((CHUNKS, SIDE, WIDE, CCOL), bf16),
            pltpu.VMEM((ZN, TOK, D), bf16),
            pltpu.VMEM((ZN, 8, TOK), f32),
            pltpu.VMEM((HALF, ROWS, D), bf16),
            pltpu.VMEM((HALF, 2 * ROWS, D), bf16),
            pltpu.VMEM((2, ROWS, D), f32),
            pltpu.VMEM((HALF, ROWS, D), bf16),
            pltpu.VMEM((HALF, ROWS, D), bf16),
            pltpu.VMEM((HALF, ROWS, D), bf16),
            pltpu.VMEM((HALF, ROWS, D), bf16),
            pltpu.VMEM((ZN, TOK, D), f32),
            pltpu.VMEM((2, HALF, TOK, D), bf16),
            pltpu.VMEM((2, HALF, TOK, D), bf16),
            dma((2,)),
            dma((2,)),
            dma((3, 3)),
            dma((CHUNKS,)),
            dma((CHUNKS,)),
            dma((CHUNKS,)),
            dma((CHUNKS,)),
            dma((CHUNKS,)),
            dma((CHUNKS,)),
            dma((CHUNKS,)),
            dma((CHUNKS,)),
            dma((2, HALF)),
            dma((2, HALF)),
            dma,
            dma,
            dma((HALF,)),
            dma((HALF,)),
            dma((HALF,)),
            dma((HALF,)),
            dma((HALF,)),
            dma((HALF,)),
            dma((HALF,)),
            dma((HALF,)),
            dma((HALF,)),
            dma((HALF,)),
            dma((2, HALF)),
            dma((2, HALF)),
        ],
        compiler_params=pltpu.CompilerParams(
            collective_id=ident, has_side_effects=True, vmem_limit_bytes=64 * 1024 * 1024 - 65536
        ),
    )(lists, length, *small, *weights)


def shards(
    frames,
    lengths,
    expert_ids,
    capacity,
    resident,
    partner,
    conv_gain,
    conv_kernel,
    conv_bias,
    ffn_gain,
    router,
    gate_weight,
    up_weight,
    down_weight,
    gate_mean_grad,
    gate_mean_square,
    up_mean_grad,
    up_mean_square,
    down_mean_grad,
    down_mean_square,
):
    lists = plan(partner)
    operands = (
        lists,
        lengths,
        (
            frames,
            expert_ids.T,
            resident[None],
            capacity[None],
            conv_gain[None],
            conv_kernel,
            conv_bias[None],
            ffn_gain[None],
            router.T,
        ),
        (
            gate_weight[0], gate_mean_grad[0], gate_mean_square[0],
            up_weight[0], up_mean_grad[0], up_mean_square[0],
            down_weight[0], down_mean_grad[0], down_mean_square[0],
        ),
    )
    block_out, fresh_gate, fresh_up, fresh_down = lax.switch(
        lists[2, 0],
        [
            lambda operands, cap=cap, ident=ident: communicate(cap, ident, *operands)
            for ident, cap in enumerate(CAPS)
        ],
        operands,
    )
    block_out, fresh_gate, fresh_up, fresh_down = write_outputs(
        (block_out, fresh_gate, fresh_up, fresh_down)
    )
    return (block_out, fresh_gate[None], fresh_up[None], fresh_down[None])


def solution(mesh):
    placed = (
        P(("dp", "expert"), None),
        P("dp"),
        P(("dp", "expert"), None),
        P(),
        P(),
        P(),
        P(),
        P(),
        P(),
        P(),
        P(),
        P("expert", None, "dp"),
        P("expert", None, "dp"),
        P("expert", None, "dp"),
        P("expert", None, "dp"),
        P("expert", None, "dp"),
        P("expert", None, "dp"),
        P("expert", None, "dp"),
        P("expert", None, "dp"),
        P("expert", None, "dp"),
    )
    return jax.shard_map(
        shards,
        mesh=mesh,
        in_specs=placed,
        out_specs=(
            P(("dp", "expert"), None),
            P("expert", None, "dp"),
            P("expert", None, "dp"),
            P("expert", None, "dp"),
        ),
        check_vma=False,
    )
```
